128 devices in a mesh: seq: 16 (over x_lo, z, core), head: 8 (over x_hi, y).
Axes of the slice: x: 4 (x_hi: 2, x_lo: 2; x = x_hi * 2 + x_lo), y: 4, z: 4, core: 2. Of those that a mesh axis runs over, the one named last changes fastest.
Arguments:
- video_query: bfloat16 [16384, 3072], P(('seq', 'head')), may hold values from -8 to 8
- video_key: bfloat16 [16384, 3072], P(('seq', 'head')), may hold values from -8 to 8
- video_value: bfloat16 [16384, 3072], P(('seq', 'head')), may hold values from -6 to 6
- video_grad: bfloat16 [16384, 3072], P(('seq', 'head')), may hold values from -6 to 6
- text_query: bfloat16 [256, 3072], P(None, 'head'), may hold values from -8 to 8
- text_key: bfloat16 [256, 3072], P(None, 'head'), may hold values from -8 to 8
- text_value: bfloat16 [256, 3072], P(None, 'head'), may hold values from -6 to 6
- text_grad: bfloat16 [256, 3072], P(None, 'head'), may hold values from -6 to 6
- tile_list: int32 [128, 8], replicated, may hold values from 0 to 127, as said below
- tile_count: int32 [128], replicated, may hold values from 1 to 8, as said below
- text_mask: int32 [256], replicated, may hold values from 0 to 1, as said below
Outputs:
- attended_video: bfloat16 [16384, 3072], P(('seq', 'head'))
- video_query_grad: bfloat16 [16384, 3072], P(('seq', 'head'))
- video_key_grad: bfloat16 [16384, 3072], P(('seq', 'head'))
- video_value_grad: bfloat16 [16384, 3072], P(('seq', 'head'))
- attended_text: bfloat16 [256, 3072], P(None, 'head')
- text_query_grad: bfloat16 [256, 3072], P(None, 'head')
- text_key_grad: bfloat16 [256, 3072], P(None, 'head')
- text_value_grad: bfloat16 [256, 3072], P(None, 'head')
The draws below stay inside these ranges and needn't reach their ends.
Inputs may be any that keep to these rules, and one draw needn't show every extreme that they name: `tile_list`: the 8 entries of one query tile's list are distinct. Query tiles fall in aligned blocks of 8; the used entries of one block together name at most 2 distinct tiles of any other block of 8 tiles, and every block names exactly 2 from some other block. `tile_count`: every aligned block of 8 query tiles has a tile that uses all 8 entries. `text_mask`: the ones form a prefix of at least 64 entries.
All inputs are finite; a program needn't handle non-finite values.
Results may differ from the reference program's by a relative error of at most 0.012.
Values may be sent and summed in bfloat16 or wider, within the bound.
No kernel may reach another device: no remote copies, remote signals or barrier semaphores. Data moves between devices by JAX's collectives and lax.ppermute only.
A program may use at most 192 MiB of HBM per device.

```python
from functools import partial
import jax
import jax.numpy as jnp
from jax import lax

H = 24
HD = 128
D = 3072
TXT = 256
TILE = 128
KT = 8
MOST = 2
VID = 16384
QT = 128
TPS = 8


def drawn_rows(key, own_key, row_total):
    normal_part = jax.random.normal(jax.random.fold_in(own_key, 17), (row_total, D), jnp.float32)
    normal_part = jnp.clip(normal_part, -8.0, 8.0)
    return normal_part


def draw_video_query(key, part):
    return drawn_rows(key, jax.random.fold_in(key, 101), VID).astype(jnp.bfloat16)


def draw_text_query(key, part):
    return drawn_rows(key, jax.random.fold_in(key, 202), TXT).astype(jnp.bfloat16)


def draw_video_key(key, part):
    own_key = jax.random.fold_in(key, 404)
    normal_part = jax.random.normal(own_key, (VID, D), jnp.float32)
    normal_part = jnp.clip(normal_part, -6.0, 6.0)
    return normal_part.astype(jnp.bfloat16)


def draw_text_key(key, part):
    own_key = jax.random.fold_in(key, 303)
    normal_part = jnp.clip(jax.random.normal(own_key, (TXT, D), jnp.float32), -8.0, 8.0)
    return normal_part.astype(jnp.bfloat16)


def tile_plan(key):
    key = jax.random.fold_in(key, 4242)
    groups = QT // TPS
    width_all = TPS + groups * MOST
    keys_split = jax.random.split(key, 5)
    raw = jax.random.randint(keys_split[0], (groups, groups, TPS), 0, 1 << 20)
    order = jnp.argsort(raw * TPS + jnp.arange(TPS), axis=-1)
    offered = order[:, :, :MOST] + (jnp.arange(groups) * TPS)[None, :, None]
    local_tiles = (jnp.arange(groups) * TPS)[:, None] + jnp.arange(TPS)[None, :]
    pool = jnp.concatenate([local_tiles, offered.reshape(groups, groups * MOST)], axis=1)
    source = jnp.concatenate([jnp.broadcast_to(jnp.arange(groups)[:, None], (groups, TPS)), jnp.broadcast_to(jnp.arange(groups)[None, :, None], (groups, groups, MOST)).reshape(groups, groups * MOST)], axis=1)
    is_slot = jnp.arange(width_all) >= TPS
    usable = jnp.logical_not(is_slot[None, :] & (source == jnp.arange(groups)[:, None]))
    chosen_tile = jax.random.randint(keys_split[1], (groups,), 0, TPS)
    chosen_source = (jnp.arange(groups) + jax.random.randint(keys_split[2], (groups,), 1, groups)) % groups
    scores = jax.random.randint(keys_split[3], (groups, TPS, width_all), 0, 1 << 12) * width_all + jnp.arange(width_all)
    forced = (jnp.arange(TPS)[None, :, None] == chosen_tile[:, None, None]) & (source[:, None, :] == chosen_source[:, None, None]) & is_slot[None, None, :]
    scores = jnp.where(forced, jnp.arange(width_all) - width_all, scores)
    scores = jnp.where(usable[:, None, :], scores, (1 << 12) * width_all + jnp.arange(width_all))
    picked = jnp.argsort(scores, axis=-1)[:, :, :KT]
    lists = jnp.take_along_axis(jnp.broadcast_to(pool[:, None, :], (groups, TPS, width_all)), picked, axis=-1).reshape(QT, KT)
    counts = jax.random.randint(keys_split[4], (groups, TPS), 1, KT + 1)
    counts = jnp.where(jnp.arange(TPS)[None, :] == chosen_tile[:, None], KT, counts).reshape(QT)
    return (lists.astype(jnp.int32), counts.astype(jnp.int32))


def draw_tile_list(key, part):
    return tile_plan(key)[0]


def draw_tile_count(key, part):
    return tile_plan(key)[1]


def draw_text_mask(key, part):
    keep = jax.random.randint(jax.random.fold_in(key, 505), (), TXT // 4, TXT + 1)
    return (jnp.arange(TXT) < keep).astype(jnp.int32)


def block_scale(stream_key, extent, cuts, low, largest):
    gain, own = 1.0, jax.random.fold_in(stream_key, 6)
    for dim, shards_of in cuts:
        steps = jnp.exp(jax.random.uniform(jax.random.fold_in(own, dim), (shards_of,), jnp.float32, low / len(cuts), largest / len(cuts)))
        gain = gain * jnp.repeat(steps, extent[dim] // shards_of).reshape([-1 if axis == dim else 1 for axis in range(len(extent))])
    return gain


def bell_draw(rng, shape, deviation, most, pieces=(), held_as=jnp.bfloat16):
    result = deviation * jax.random.normal(rng, shape, jnp.float32)
    if pieces:
        result = result * block_scale(rng, shape, pieces, -0.22, 0.18)
    return jnp.clip(result, -most, most).astype(held_as)


def setup_inputs(seed: int = 0) -> dict:
    splits = jax.random.split(jax.random.key(seed), 12)
    video_query = draw_video_query(jax.random.fold_in(splits[11], 71), 0)
    video_key = draw_video_key(jax.random.fold_in(splits[11], 71), 0)
    video_value = bell_draw(splits[2], (VID, D), 1.0, 6.0, ((0, 128),))
    video_grad = bell_draw(splits[3], (VID, D), 1.0, 6.0, ((0, 128),))
    text_query = draw_text_query(jax.random.fold_in(splits[11], 71), 0)
    text_key = draw_text_key(jax.random.fold_in(splits[11], 71), 0)
    text_value = bell_draw(splits[6], (TXT, D), 1.0, 6.0, ((1, 8),))
    text_grad = bell_draw(splits[7], (TXT, D), 1.0, 6.0, ((1, 8),))
    tile_list = draw_tile_list(jax.random.fold_in(splits[11], 71), 0)
    tile_count = draw_tile_count(jax.random.fold_in(splits[11], 71), 0)
    text_mask = draw_text_mask(jax.random.fold_in(splits[11], 71), 0)
    return dict(video_query=video_query, video_key=video_key, video_value=video_value, video_grad=video_grad, text_query=text_query, text_key=text_key, text_value=text_value, text_grad=text_grad, tile_list=tile_list, tile_count=tile_count, text_mask=text_mask)


NEGATIVE = -1.0e30
HIGHEST_PRECISION = lax.Precision.HIGHEST


def per_head(arrays, tile_list, tile_count, text_ok):
    query_vid, key_vid, value_vid, grad_vid, query_txt, key_txt, value_txt, grad_txt = arrays
    factor = HD ** -0.5
    key_tiles = key_vid.reshape(QT, TILE, HD)
    value_tiles = value_vid.reshape(QT, TILE, HD)

    def step(running, tile_index):
        key_acc, value_acc, text_key_acc, text_value_acc = running
        query_rows = lax.dynamic_slice_in_dim(query_vid, tile_index * TILE, TILE, 0)
        grad_rows = lax.dynamic_slice_in_dim(grad_vid, tile_index * TILE, TILE, 0)
        listed = tile_list[tile_index]
        key_rows = jnp.concatenate([key_tiles[listed].reshape(KT * TILE, HD), key_txt], axis=0)
        value_rows = jnp.concatenate([value_tiles[listed].reshape(KT * TILE, HD), value_txt], axis=0)
        live_keys = jnp.concatenate([jnp.repeat(jnp.arange(KT) < tile_count[tile_index], TILE), text_ok])
        scores = jnp.dot(query_rows, key_rows.T, preferred_element_type=jnp.float32) * factor
        scores = jnp.where(live_keys[None, :], scores, NEGATIVE)
        maximum = jnp.max(scores, axis=1, keepdims=True)
        log_total = maximum + jnp.log(jnp.sum(jnp.exp(scores - maximum), axis=1, keepdims=True))
        probability = jnp.exp(scores - log_total)
        weights = probability.astype(jnp.bfloat16)
        output = jnp.dot(weights, value_rows, preferred_element_type=jnp.float32)
        offset = jnp.sum(grad_rows.astype(jnp.float32) * output, axis=1, keepdims=True)
        prob_grad = jnp.dot(grad_rows, value_rows.T, preferred_element_type=jnp.float32)
        score_grad = (probability * (prob_grad - offset)).astype(jnp.bfloat16)
        query_grad = jnp.dot(score_grad, key_rows, preferred_element_type=jnp.float32) * factor
        key_grad = jnp.dot(score_grad.T, query_rows, preferred_element_type=jnp.float32) * factor
        value_grad = jnp.dot(weights.T, grad_rows, preferred_element_type=jnp.float32)
        key_acc = key_acc.at[listed].add(key_grad[:KT * TILE].reshape(KT, TILE, HD))
        value_acc = value_acc.at[listed].add(value_grad[:KT * TILE].reshape(KT, TILE, HD))
        text_key_acc = text_key_acc + key_grad[KT * TILE:]
        text_value_acc = text_value_acc + value_grad[KT * TILE:]
        return (key_acc, value_acc, text_key_acc, text_value_acc), (output.astype(jnp.bfloat16), query_grad.astype(jnp.bfloat16))

    start = (jnp.zeros((QT, TILE, HD), jnp.float32), jnp.zeros((QT, TILE, HD), jnp.float32),
             jnp.zeros((TXT, HD), jnp.float32), jnp.zeros((TXT, HD), jnp.float32))
    finals, outputs = lax.scan(step, start, jnp.arange(QT, dtype=jnp.int32))
    key_acc, value_acc, text_key_acc, text_value_acc = finals
    video_out = outputs[0].reshape(VID, HD)
    video_query_grad = outputs[1].reshape(VID, HD)

    key_all = jnp.concatenate([key_vid, key_txt], axis=0)
    value_all = jnp.concatenate([value_vid, value_txt], axis=0)
    live_all = jnp.concatenate([jnp.ones((VID,), bool), text_ok])
    scores = jnp.dot(query_txt, key_all.T, preferred_element_type=jnp.float32) * factor
    scores = jnp.where(live_all[None, :], scores, NEGATIVE)
    maximum = jnp.max(scores, axis=1, keepdims=True)
    log_total = maximum + jnp.log(jnp.sum(jnp.exp(scores - maximum), axis=1, keepdims=True))
    probability = jnp.exp(scores - log_total)
    text_out = jnp.dot(probability, value_all.astype(jnp.float32), precision=HIGHEST_PRECISION)
    offset = jnp.sum(grad_txt.astype(jnp.float32) * text_out, axis=1, keepdims=True)
    prob_grad = jnp.dot(grad_txt, value_all.T, preferred_element_type=jnp.float32)
    score_grad = probability * (prob_grad - offset)
    text_query_grad = jnp.dot(score_grad, key_all.astype(jnp.float32), precision=HIGHEST_PRECISION) * factor
    key_from_text = jnp.dot(score_grad.T, query_txt.astype(jnp.float32), precision=HIGHEST_PRECISION) * factor
    value_from_text = jnp.dot(probability.T, grad_txt.astype(jnp.float32), precision=HIGHEST_PRECISION)
    video_key_grad = key_acc.reshape(VID, HD) + key_from_text[:VID]
    video_value_grad = value_acc.reshape(VID, HD) + value_from_text[:VID]
    text_key_grad = text_key_acc + key_from_text[VID:]
    text_value_grad = text_value_acc + value_from_text[VID:]
    return (video_out, video_query_grad, video_key_grad.astype(jnp.bfloat16), video_value_grad.astype(jnp.bfloat16),
            text_out.astype(jnp.bfloat16), text_query_grad.astype(jnp.bfloat16),
            text_key_grad.astype(jnp.bfloat16), text_value_grad.astype(jnp.bfloat16))


def split_heads(matrix):
    return jnp.transpose(matrix.reshape(matrix.shape[0], H, HD), (1, 0, 2))


def join_heads(matrix):
    return jnp.transpose(matrix, (1, 0, 2)).reshape(matrix.shape[1], H * HD)


def reference(video_query, video_key, video_value, video_grad, text_query, text_key, text_value, text_grad, tile_list, tile_count, text_mask):
    text_ok = text_mask > 0
    stacked = tuple(split_heads(matrix) for matrix in (video_query, video_key, video_value, video_grad, text_query, text_key, text_value, text_grad))
    results = lax.map(partial(per_head, tile_list=tile_list, tile_count=tile_count, text_ok=text_ok), stacked)
    return (join_heads(results[0]), join_heads(results[1]), join_heads(results[2]), join_heads(results[3]),
            join_heads(results[4]), join_heads(results[5]), join_heads(results[6]), join_heads(results[7]))
```

```python
import functools

import jax
import jax.numpy as jnp
from jax import lax
from jax.experimental import pallas as pl
from jax.experimental.pallas import tpu as pltpu
from jax.sharding import PartitionSpec as P

HD = 128
TXT = 256
TILE = 128
KT = 8
MOST = 2
GROUPS = 16
HEADS = 8
TILES = 8
NH = 3
W = NH * HD
SLOTS = GROUPS * MOST
POOL = TILES + SLOTS
TROWS = TXT // GROUPS
TLOCAL = TILES * TILE
TCHUNKS = TLOCAL // 256 + 1
BACK = MOST * 2 * TILE + 3 * TROWS

NEGATIVE = -1e30
FACTOR = HD**-0.5
LOG2E = 1.4426950408889634
FACTOR2 = FACTOR * LOG2E
VMEM_LIMIT = 60 * 1024 * 1024

F32 = jnp.float32
BF16 = jnp.bfloat16
SMEM = pltpu.SMEM
ANY = pl.ANY


def dot_nt(a, b):
    return lax.dot_general(a, b, (((1,), (1,)), ((), ())), preferred_element_type=F32)


def dot_nn(a, b):
    return lax.dot_general(a, b, (((1,), (0,)), ((), ())), preferred_element_type=F32)


def dot_tn(a, b):
    return lax.dot_general(a, b, (((0,), (0,)), ((), ())), preferred_element_type=F32)


def params(**kw):
    return pltpu.CompilerParams(vmem_limit_bytes=VMEM_LIMIT, **kw)


def cost(flops, nbytes, exps=0):
    return pl.CostEstimate(
        flops=int(flops), bytes_accessed=int(nbytes), transcendentals=int(exps)
    )


def pack_kernel(k_ref, v_ref, q_ref, g_ref, o_ref):
    for n, ref in enumerate((k_ref, v_ref, q_ref, g_ref)):
        o_ref[0, n] = ref[...]


def pack(k, v, q, g):
    spec = pl.BlockSpec((TILE, W), lambda h: (0, h))
    return pl.pallas_call(
        pack_kernel,
        grid=(HEADS,),
        in_specs=[spec] * 4,
        out_specs=pl.BlockSpec((1, 4, TILE, W), lambda h: (h, 0, 0, 0)),
        out_shape=jax.ShapeDtypeStruct((HEADS, 4, TILE, W), BF16),
        compiler_params=params(),
        cost_estimate=cost(0, 8 * TILE * HEADS * W * 2),
        name="pack",
    )(k, v, q, g)


def unpack_kernel(x_ref, a_ref, b_ref, c_ref, d_ref):
    for n, ref in enumerate((a_ref, b_ref, c_ref, d_ref)):
        ref[...] = x_ref[0, n]


def unpack(x):
    spec = pl.BlockSpec((TILE, W), lambda h: (0, h))
    return pl.pallas_call(
        unpack_kernel,
        grid=(HEADS,),
        in_specs=[pl.BlockSpec((1, 4, TILE, W), lambda h: (h, 0, 0, 0))],
        out_specs=[spec] * 4,
        out_shape=[jax.ShapeDtypeStruct((TILE, HEADS * W), BF16)] * 4,
        compiler_params=params(),
        cost_estimate=cost(0, 8 * TILE * HEADS * W * 2),
        name="unpack",
    )(x)


def pick_kernel(sel_ref, x_ref, o_ref, sems):
    copies = [
        pltpu.make_async_copy(x_ref.at[sel_ref[s]], o_ref.at[s], sems.at[s])
        for s in range(SLOTS)
    ]
    for copy in copies:
        copy.start()
    for copy in copies:
        copy.wait()


def pick(sel, x):
    return pl.pallas_call(
        pick_kernel,
        grid=(1,),
        in_specs=[
            pl.BlockSpec(memory_space=SMEM),
            pl.BlockSpec((TILES, 2, TILE, W), lambda i: (0, 0, 0, 0)),
        ],
        out_specs=pl.BlockSpec(memory_space=ANY),
        out_shape=jax.ShapeDtypeStruct((SLOTS, 2, TILE, W), BF16),
        scratch_shapes=[pltpu.SemaphoreType.DMA((SLOTS,))],
        compiler_params=params(),
        cost_estimate=cost(0, (SLOTS + TILES) * 2 * TILE * W * 2),
        name="pick",
    )(sel, x)


def text_chunk(x_ref, text_ref, which, c, lanes):
    if c < TCHUNKS - 1:
        return x_ref[2 * c : 2 * c + 2, which, :, lanes].reshape(256, HD)
    return text_ref[:, lanes]


def head_lanes(j):
    return pl.ds(pl.multiple_of(j * HD, HD), HD)


def text_forward_kernel(n_ref, tq_ref, tk_ref, tv_ref, x_ref, o_ref, s_ref):
    live = lax.broadcasted_iota(jnp.int32, (TXT, TXT), 1) < n_ref[0]
    lane = lax.broadcasted_iota(jnp.int32, (TXT, HD), 1)
    o_ref[:, W:] = jnp.zeros((TXT, HD), F32)

    def head(j, carry):
        lanes = head_lanes(j)
        query = tq_ref[:, lanes]
        top = None
        for c in range(TCHUNKS):
            s = dot_nt(query, text_chunk(x_ref, tk_ref, 0, c, lanes)) * FACTOR2
            if c == TCHUNKS - 1:
                s = jnp.where(live, s, NEGATIVE)
            s_ref[c] = s
            top = s if top is None else jnp.maximum(top, s)
        top = jnp.max(top, axis=1, keepdims=True)
        total, out = None, None
        for c in range(TCHUNKS):
            p = jnp.exp2(s_ref[c] - top)
            part = dot_nn(p.astype(BF16), text_chunk(x_ref, tv_ref, 1, c, lanes))
            total = p if total is None else total + p
            out = part if out is None else out + part
        total = jnp.sum(total, axis=1, keepdims=True)
        o_ref[:, lanes] = out
        stats = o_ref[:, W:]
        stats = jnp.where(lane == j, top, stats)
        o_ref[:, W:] = jnp.where(lane == j + 8, total, stats)
        return carry

    lax.fori_loop(0, NH, head, 0)


def whole(shape):
    return pl.BlockSpec(shape, lambda i: (0,) * len(shape))


TEXT = (TXT, W)
LOCAL_KV = (TILES, 2, TILE, W)


def text_forward(n, tq, tk, tv, x):
    return pl.pallas_call(
        text_forward_kernel,
        grid=(1,),
        in_specs=[pl.BlockSpec(memory_space=SMEM)] + [whole(TEXT)] * 3 + [whole(LOCAL_KV)],
        out_specs=whole((TXT, W + HD)),
        out_shape=jax.ShapeDtypeStruct((TXT, W + HD), F32),
        scratch_shapes=[pltpu.VMEM((TCHUNKS, TXT, 256), F32)],
        compiler_params=params(),
        cost_estimate=cost(4 * NH * TXT * TCHUNKS * 256 * HD, 3 << 20, NH * TXT * 1280),
        name="text_forward",
    )(n, tq, tk, tv, x)


def merged(flag_ref, a_ref, b_ref, j, lanes):
    swap = flag_ref[0] > 0
    stats_a = jnp.where(swap, b_ref[:, W:], a_ref[:, W:])
    stats_b = jnp.where(swap, a_ref[:, W:], b_ref[:, W:])
    lane = lax.broadcasted_iota(jnp.int32, (TXT, HD), 1)

    def column(stats, at):
        return jnp.sum(jnp.where(lane == at, stats, 0.0), axis=1, keepdims=True)

    top_a, top_b = column(stats_a, j), column(stats_b, j)
    top = jnp.maximum(top_a, top_b)
    scale_a, scale_b = jnp.exp2(top_a - top), jnp.exp2(top_b - top)
    total = column(stats_a, j + 8) * scale_a + column(stats_b, j + 8) * scale_b
    out_a = jnp.where(swap, b_ref[:, lanes], a_ref[:, lanes])
    out_b = jnp.where(swap, a_ref[:, lanes], b_ref[:, lanes])
    out = out_a * scale_a + out_b * scale_b
    return top, total, out


def text_merge_kernel(flag_ref, a_ref, b_ref, o_ref):
    lane = lax.broadcasted_iota(jnp.int32, (TXT, HD), 1)
    stats = jnp.zeros((TXT, HD), F32)
    for j in range(NH):
        lanes = slice(j * HD, (j + 1) * HD)
        top, total, out = merged(flag_ref, a_ref, b_ref, j, lanes)
        o_ref[:, lanes] = out
        stats = jnp.where(lane == j, top, stats)
        stats = jnp.where(lane == j + 8, total, stats)
    o_ref[:, W:] = stats


def text_merge(flag, a, b):
    return pl.pallas_call(
        text_merge_kernel,
        grid=(1,),
        in_specs=[pl.BlockSpec(memory_space=SMEM)] + [whole((TXT, W + HD))] * 2,
        out_specs=whole((TXT, W + HD)),
        out_shape=jax.ShapeDtypeStruct((TXT, W + HD), F32),
        compiler_params=params(),
        cost_estimate=cost(TXT * W * 4, 3 * TXT * (W + HD) * 4),
        name="text_merge",
    )(flag, a, b)


def text_backward_kernel(
    n_ref, flag_ref, a_ref, b_ref, tq_ref, tk_ref, tv_ref, tg_ref, x_ref, out_ref, tqg_ref, acc_ref, dx_ref
):
    live = lax.broadcasted_iota(jnp.int32, (TXT, TXT), 1) < n_ref[0]

    def head(j, carry):
        lanes = head_lanes(j)
        top, total, out = merged(flag_ref, a_ref, b_ref, j, lanes)
        out = out / total
        out_ref[:, lanes] = out.astype(BF16)
        log_total = top + jnp.log2(total)
        query, grad = tq_ref[:, lanes], tg_ref[:, lanes]
        offset = jnp.sum(grad.astype(F32) * out, axis=1, keepdims=True)
        query_grad = None
        for c in range(TCHUNKS):
            key = text_chunk(x_ref, tk_ref, 0, c, lanes)
            value = text_chunk(x_ref, tv_ref, 1, c, lanes)
            s = dot_nt(query, key) * FACTOR2
            if c == TCHUNKS - 1:
                s = jnp.where(live, s, NEGATIVE)
            p = jnp.exp2(s - log_total)
            ds = (p * (dot_nt(grad, value) - offset)).astype(BF16)
            p = p.astype(BF16)
            part = dot_nn(ds, key)
            query_grad = part if query_grad is None else query_grad + part
            key_grad = dot_tn(ds, query)
            value_grad = dot_tn(p, grad)
            if c < TCHUNKS - 1:
                dx_ref[2 * c : 2 * c + 2, 0, :, lanes] = key_grad.reshape(2, TILE, HD)
                dx_ref[2 * c : 2 * c + 2, 1, :, lanes] = value_grad.reshape(2, TILE, HD)
            else:
                acc_ref[0, :, lanes] = key_grad
                acc_ref[1, :, lanes] = value_grad
        tqg_ref[:, lanes] = query_grad * FACTOR
        return carry

    lax.fori_loop(0, NH, head, 0)


def text_backward(n, flag, a, b, tq, tk, tv, tg, x):
    return pl.pallas_call(
        text_backward_kernel,
        grid=(1,),
        in_specs=[pl.BlockSpec(memory_space=SMEM)] * 2
        + [whole((TXT, W + HD))] * 2
        + [whole(TEXT)] * 4
        + [whole(LOCAL_KV)],
        out_specs=[whole(TEXT), whole(TEXT), whole((2, TXT, W)), whole(LOCAL_KV)],
        out_shape=[
            jax.ShapeDtypeStruct(TEXT, BF16),
            jax.ShapeDtypeStruct(TEXT, F32),
            jax.ShapeDtypeStruct((2, TXT, W), F32),
            jax.ShapeDtypeStruct(LOCAL_KV, F32),
        ],
        compiler_params=params(),
        cost_estimate=cost(10 * NH * TXT * TCHUNKS * 256 * HD, 8 << 20, NH * TXT * 1280),
        name="text_backward",
    )(n, flag, a, b, tq, tk, tv, tg, x)


CHUNKS = KT // 2 + 1


def video_kernel(
    slot_ref,
    count_ref,
    n_ref,
    kv_ref,
    qg_ref,
    got_ref,
    tk_ref,
    tv_ref,
    tqg_ref,
    tacc_ref,
    dx_ref,
    out_ref,
    back_ref,
    own_ref,
    keys,
    values,
    s_ref,
    p_ref,
    dk_acc,
    dv_acc,
    tk_acc,
    tv_acc,
    pool,
):
    pool[:TILES] = kv_ref[...]
    pool[TILES:] = got_ref[...]
    keys[0] = tk_ref[...]
    values[0] = tv_ref[...]
    dk_acc[:TILES] = dx_ref[:, 0]
    dv_acc[:TILES] = dx_ref[:, 1]
    dk_acc[TILES:] = jnp.zeros((SLOTS, TILE, HD), F32)
    dv_acc[TILES:] = jnp.zeros((SLOTS, TILE, HD), F32)
    tk_acc[...] = tacc_ref[0]
    tv_acc[...] = tacc_ref[1]
    text_live = lax.broadcasted_iota(jnp.int32, (TXT, TILE), 0) < n_ref[0]

    def tile(i, carry):
        count = count_ref[i]
        query, grad = qg_ref[i, 0], qg_ref[i, 1]

        def run(pairs):
            slots = [slot_ref[i * KT + e] for e in range(2 * pairs)]
            for e in range(2 * pairs):
                half = pl.ds((e % 2) * TILE, TILE)
                keys[1 + e // 2, half] = pool[slots[e], 0]
                values[1 + e // 2, half] = pool[slots[e], 1]
            top = None
            for c in range(pairs + 1):
                s = dot_nt(keys[c], query) * FACTOR2
                if c == 0:
                    s = jnp.where(text_live, s, NEGATIVE)
                elif c == pairs:
                    s = jnp.concatenate(
                        [s[:TILE], jnp.where(2 * pairs <= count, s[TILE:], NEGATIVE)], axis=0
                    )
                s_ref[c] = s
                part = jnp.max(s.reshape(32, 8, TILE), axis=0)
                top = part if top is None else jnp.maximum(top, part)
            top = jnp.max(top, axis=0, keepdims=True)
            total = None
            for c in range(pairs + 1):
                p = jnp.exp2(s_ref[c] - top)
                s_ref[c] = p
                part = jnp.sum(p.reshape(32, 8, TILE), axis=0)
                total = part if total is None else total + part
            scale = 1.0 / jnp.sum(total, axis=0, keepdims=True)
            out = None
            for c in range(pairs + 1):
                p = s_ref[c] * scale
                s_ref[c] = p
                p = p.astype(BF16)
                p_ref[c] = p
                part = dot_tn(p, values[c])
                out = part if out is None else out + part
            out_ref[i, 0] = out.astype(BF16)
            offset = jnp.sum((grad.astype(F32) * out).T, axis=0, keepdims=True)
            query_grad = None
            for c in range(pairs + 1):
                ds = (s_ref[c] * (dot_nt(values[c], grad) - offset)).astype(BF16)
                part = dot_tn(ds, keys[c])
                query_grad = part if query_grad is None else query_grad + part
                key_grad = dot_nn(ds, query)
                value_grad = dot_nn(p_ref[c], grad)
                if c == 0:
                    tk_acc[...] += key_grad
                    tv_acc[...] += value_grad
                else:
                    for e in (0, 1):
                        slot = slots[2 * (c - 1) + e]
                        dk_acc[slot] += key_grad[e * TILE : (e + 1) * TILE]
                        dv_acc[slot] += value_grad[e * TILE : (e + 1) * TILE]
            out_ref[i, 1] = (query_grad * FACTOR).astype(BF16)

        for pairs in range(1, KT // 2 + 1):

            @pl.when((count + 1) // 2 == pairs)
            def _():
                run(pairs)

        return carry

    lax.fori_loop(0, TILES, tile, 0)

    own_ref[:, 0] = dk_acc[:TILES]
    own_ref[:, 1] = dv_acc[:TILES]
    for g in range(GROUPS):
        for m in range(MOST):
            slot = TILES + g * MOST + m
            back_ref[g, 2 * m * TILE : (2 * m + 1) * TILE] = (dk_acc[slot] * FACTOR).astype(BF16)
            back_ref[g, (2 * m + 1) * TILE : (2 * m + 2) * TILE] = dv_acc[slot].astype(BF16)
        rows = slice(g * TROWS, (g + 1) * TROWS)
        at = MOST * 2 * TILE
        back_ref[g, at : at + TROWS] = tqg_ref[rows].astype(BF16)
        back_ref[g, at + TROWS : at + 2 * TROWS] = (tk_acc[rows] * FACTOR).astype(BF16)
        back_ref[g, at + 2 * TROWS : at + 3 * TROWS] = tv_acc[rows].astype(BF16)


def video(slot, count, n, x, got, tk, tv, tqg, tacc, dx):
    smem = pl.BlockSpec(memory_space=SMEM)
    text = pl.BlockSpec((TXT, HD), lambda j: (0, j))
    pair = (TILES, 2, TILE, HD)
    return pl.pallas_call(
        video_kernel,
        grid=(NH,),
        in_specs=[
            smem,
            smem,
            smem,
            pl.BlockSpec(pair, lambda j: (0, 0, 0, j)),
            pl.BlockSpec(pair, lambda j: (0, 1, 0, j)),
            pl.BlockSpec((SLOTS, 2, TILE, HD), lambda j: (0, 0, 0, j)),
            text,
            text,
            text,
            pl.BlockSpec((2, TXT, HD), lambda j: (0, 0, j)),
            pl.BlockSpec(pair, lambda j: (0, 0, 0, j)),
        ],
        out_specs=[
            pl.BlockSpec(pair, lambda j: (0, 0, 0, j)),
            pl.BlockSpec((GROUPS, BACK, HD), lambda j: (0, 0, j)),
            pl.BlockSpec(pair, lambda j: (0, 0, 0, j)),
        ],
        out_shape=[
            jax.ShapeDtypeStruct((TILES, 2, TILE, W), BF16),
            jax.ShapeDtypeStruct((GROUPS, BACK, W), BF16),
            jax.ShapeDtypeStruct((TILES, 2, TILE, W), F32),
        ],
        scratch_shapes=[
            pltpu.VMEM((CHUNKS, 256, HD), BF16),
            pltpu.VMEM((CHUNKS, 256, HD), BF16),
            pltpu.VMEM((CHUNKS, 256, TILE), F32),
            pltpu.VMEM((CHUNKS, 256, TILE), BF16),
            pltpu.VMEM((POOL, TILE, HD), F32),
            pltpu.VMEM((POOL, TILE, HD), F32),
            pltpu.VMEM((TXT, HD), F32),
            pltpu.VMEM((TXT, HD), F32),
            pltpu.VMEM((POOL, 2, TILE, HD), BF16),
        ],
        compiler_params=params(),
        cost_estimate=cost(12 * NH * TLOCAL * 1280 * HD, 24 << 20, NH * TLOCAL * 1280),
        name="video",
    )(slot, count, n, x, x, got, tk, tv, tqg, tacc, dx)


def combine_kernel(sel_ref, back_ref, own_ref, half_ref, out_ref, text_ref, acc):
    acc[:, 0] = own_ref[:, 0] * FACTOR
    acc[:, 1] = own_ref[:, 1]

    def add(g, carry):
        for m in range(MOST):
            at = sel_ref[g * MOST + m]
            part = back_ref[g, 2 * m * TILE : 2 * (m + 1) * TILE].astype(F32)
            acc[at] += part.reshape(2, TILE, HD)
        return carry

    lax.fori_loop(0, GROUPS, add, 0)
    out_ref[:, :2] = half_ref[...]
    out_ref[:, 2:] = acc[...].astype(BF16)
    text = None
    for g in range(GROUPS):
        part = back_ref[g, MOST * 2 * TILE :].astype(F32)
        text = part if text is None else text + part
    text_ref[...] = text.astype(BF16)


def combine(sel, back, own, half):
    pair = (TILES, 2, TILE, HD)
    return pl.pallas_call(
        combine_kernel,
        grid=(NH,),
        in_specs=[
            pl.BlockSpec(memory_space=SMEM),
            pl.BlockSpec((GROUPS, BACK, HD), lambda j: (0, 0, j)),
            pl.BlockSpec(pair, lambda j: (0, 0, 0, j)),
            pl.BlockSpec(pair, lambda j: (0, 0, 0, j)),
        ],
        out_specs=[
            pl.BlockSpec((TILES, 4, TILE, HD), lambda j: (0, 0, 0, j)),
            pl.BlockSpec((3 * TROWS, HD), lambda j: (0, j)),
        ],
        out_shape=[
            jax.ShapeDtypeStruct((TILES, 4, TILE, W), BF16),
            jax.ShapeDtypeStruct((3 * TROWS, W), BF16),
        ],
        scratch_shapes=[pltpu.VMEM(pair, F32)],
        compiler_params=params(),
        cost_estimate=cost(TLOCAL * W * 64, 16 << 20),
        name="combine",
    )(sel, back, own, half)


STEPS = ((1, 1), (2, 2), (4, 6), (8, 8))


def swapped(x, mask):
    return lax.ppermute(x, "seq", [(i, i ^ mask) for i in range(GROUPS)])


def tables(tile_list, tile_count, own):
    live = jnp.arange(KT)[None, :] < tile_count[:, None]
    listed = jnp.where(live, tile_list, -1)

    def ranked(wanted):
        before = jnp.arange(TILES)[:, None] < jnp.arange(TILES)[None, :]
        return jnp.sum(jnp.where(before[None], wanted[:, :, None], 0), axis=1)

    mine = own * TILES + jnp.arange(TILES)
    asked = jnp.any(
        listed.reshape(GROUPS, TILES * KT, 1) == mine[None, None, :], axis=1
    ).astype(jnp.int32)
    rank = ranked(asked)
    chosen = (asked[:, None, :] > 0) & (rank[:, None, :] == jnp.arange(MOST)[None, :, None])
    sel = jnp.sum(jnp.where(chosen, jnp.arange(TILES)[None, None, :], 0), axis=2).reshape(SLOTS)

    my_list = lax.dynamic_slice_in_dim(listed, own * TILES, TILES, 0).reshape(TILES * KT)
    hits = my_list[:, None] == jnp.arange(GROUPS * TILES)[None, :]
    needed = jnp.any(hits, axis=0).astype(jnp.int32).reshape(GROUPS, TILES)
    where_to = TILES + jnp.arange(GROUPS)[:, None] * MOST + jnp.minimum(ranked(needed), MOST - 1)
    local = jnp.arange(GROUPS)[:, None] == own
    where_to = jnp.where(local, jnp.arange(TILES)[None, :], where_to).reshape(GROUPS * TILES)
    slot = jnp.sum(jnp.where(hits, where_to[None, :], 0), axis=1)
    count = lax.dynamic_slice_in_dim(tile_count, own * TILES, TILES, 0)
    return sel.astype(jnp.int32), slot.astype(jnp.int32), count.astype(jnp.int32)


def body(
    video_query,
    video_key,
    video_value,
    video_grad,
    text_query,
    text_key,
    text_value,
    text_grad,
    tile_list,
    tile_count,
    text_mask,
):
    own = lax.axis_index("seq")
    x = lax.all_to_all(
        pack(video_key, video_value, video_query, video_grad), "head", 0, 0, tiled=True
    )
    sel, slot, count = tables(tile_list, tile_count, own)
    n = jnp.sum((text_mask > 0).astype(jnp.int32)).reshape(1)
    n_own = jnp.where(own == 0, n, 0)

    got = lax.all_to_all(
        pick(sel, x).reshape(GROUPS, MOST * 2 * TILE, W), "seq", 0, 0, tiled=True
    ).reshape(SLOTS, 2, TILE, W)

    part = text_forward(n_own, text_query, text_key, text_value, x)
    upper = [((own & bit) > 0).astype(jnp.int32).reshape(1) for bit, _ in STEPS]
    for flag, (_, mask) in zip(upper[:-1], STEPS[:-1]):
        part = text_merge(flag, part, swapped(part, mask))
    other = swapped(part, STEPS[-1][1])
    attended_text, tqg, tacc, dx = text_backward(
        n_own, upper[-1], part, other, text_query, text_key, text_value, text_grad, x
    )

    half, back, own_grads = video(slot, count, n, x, got, text_key, text_value, tqg, tacc, dx)
    back = lax.all_to_all(back, "seq", 0, 0, tiled=True)
    packed, text_rows = combine(sel, back, own_grads, half)

    gathered = text_rows.reshape(1, 3, TROWS, W)
    for bit, mask in STEPS:
        theirs = swapped(gathered, mask)
        first = jnp.concatenate([gathered, theirs], axis=0)
        second = jnp.concatenate([theirs, gathered], axis=0)
        gathered = jnp.where((own & bit) == 0, first, second)
    text_grads = jnp.transpose(gathered, (1, 0, 2, 3)).reshape(3, TXT, W)

    attended_video, video_query_grad, video_key_grad, video_value_grad = unpack(
        lax.all_to_all(packed, "head", 0, 0, tiled=True)
    )
    return (
        attended_video,
        video_query_grad,
        video_key_grad,
        video_value_grad,
        attended_text,
        text_grads[0],
        text_grads[1],
        text_grads[2],
    )


def solution(mesh):
    tokens, heads = P(("seq", "head"), None), P(None, "head")
    return jax.shard_map(
        body,
        mesh=mesh,
        in_specs=(tokens,) * 4 + (heads,) * 4 + (P(),) * 3,
        out_specs=(tokens,) * 4 + (heads,) * 4,
        check_vma=False,
    )
```

```python
import functools

import jax
import jax.numpy as jnp
from jax import lax
from jax.experimental import pallas as pl
from jax.experimental.pallas import tpu as pltpu
from jax.sharding import PartitionSpec as P

HD = 128
TXT = 256
TILE = 128
KT = 8
MOST = 2
GROUPS = 16
HEADS = 8
TILES = 8
NH = 3
W = NH * HD
SLOTS = GROUPS * MOST
POOL = TILES + SLOTS
TROWS = TXT // GROUPS
TLOCAL = TILES * TILE
TCHUNKS = TLOCAL // 256 + 1
PAIR_ROWS = MOST * 2 * TILE
SEND_FIRST = PAIR_ROWS + 2 * TROWS
SEND_REST = PAIR_ROWS + TROWS
BACK_REST = PAIR_ROWS + 3 * NH * TROWS
NF = 2
WF = NF * HD
WR = W - WF

NEGATIVE = -1e30
FACTOR = HD**-0.5
LOG2E = 1.4426950408889634
FACTOR2 = FACTOR * LOG2E
VMEM_LIMIT = 67043328

F32 = jnp.float32
BF16 = jnp.bfloat16
SMEM = pltpu.SMEM
ANY = pl.ANY


def dot_nt(a, b):
    return lax.dot_general(a, b, (((1,), (1,)), ((), ())), preferred_element_type=F32)


def dot_nn(a, b):
    return lax.dot_general(a, b, (((1,), (0,)), ((), ())), preferred_element_type=F32)


def dot_tn(a, b):
    return lax.dot_general(a, b, (((0,), (0,)), ((), ())), preferred_element_type=F32)


def params(**kw):
    return pltpu.CompilerParams(vmem_limit_bytes=VMEM_LIMIT, **kw)


def cost(flops, nbytes, exps=0):
    return pl.CostEstimate(
        flops=int(flops), bytes_accessed=int(nbytes), transcendentals=int(exps)
    )


def go(copies):
    for copy in copies:
        copy.start()
    return copies


def finish(copies):
    for copy in copies:
        copy.wait()


def columns(h):
    return pl.ds(h * W, W)


def pack_kernel(k_ref, v_ref, q_ref, g_ref, o_ref, rows, in_sems, out_sems):
    refs = (k_ref, v_ref, q_ref, g_ref)
    loads = go([pltpu.make_async_copy(refs[n], rows.at[n], in_sems.at[n]) for n in range(4)])
    stores = []
    for n in range(4):
        loads[n].wait()
        stores += go(
            [
                pltpu.make_async_copy(
                    rows.at[n, :, columns(h)], o_ref.at[h, n], out_sems.at[n, h]
                )
                for h in range(HEADS)
            ]
        )
    finish(stores)


def any_specs(n):
    return [pl.BlockSpec(memory_space=ANY)] * n


def pack(k, v, q, g):
    return pl.pallas_call(
        pack_kernel,
        in_specs=any_specs(4),
        out_specs=pl.BlockSpec(memory_space=ANY),
        out_shape=jax.ShapeDtypeStruct((HEADS, 4, TILE, W), BF16),
        scratch_shapes=[
            pltpu.VMEM((4, TILE, HEADS * W), BF16),
            pltpu.SemaphoreType.DMA((4,)),
            pltpu.SemaphoreType.DMA((4, HEADS)),
        ],
        compiler_params=params(),
        cost_estimate=cost(0, 8 * TILE * HEADS * W * 2),
        name="pack",
    )(k, v, q, g)


def unpack_kernel(x_ref, a_ref, b_ref, c_ref, d_ref, rows, in_sems, out_sems):
    refs = (a_ref, b_ref, c_ref, d_ref)
    loads = [
        go(
            [
                pltpu.make_async_copy(
                    x_ref.at[h, n], rows.at[n, :, columns(h)], in_sems.at[n, h]
                )
                for h in range(HEADS)
            ]
        )
        for n in range(4)
    ]
    stores = []
    for n in range(4):
        finish(loads[n])
        stores += go([pltpu.make_async_copy(rows.at[n], refs[n], out_sems.at[n])])
    finish(stores)


def unpack(x):
    return pl.pallas_call(
        unpack_kernel,
        in_specs=any_specs(1),
        out_specs=any_specs(4),
        out_shape=[jax.ShapeDtypeStruct((TILE, HEADS * W), BF16)] * 4,
        scratch_shapes=[
            pltpu.VMEM((4, TILE, HEADS * W), BF16),
            pltpu.SemaphoreType.DMA((4, HEADS)),
            pltpu.SemaphoreType.DMA((4,)),
        ],
        compiler_params=params(),
        cost_estimate=cost(0, 8 * TILE * HEADS * W * 2),
        name="unpack",
    )(x)


def picked(sel_ref, x_ref, o_ref, sems, lanes):
    return [
        pltpu.make_async_copy(
            x_ref.at[sel_ref[g * MOST + m], kv, :, lanes],
            o_ref.at[g, pl.ds((2 * m + kv) * TILE, TILE)],
            sems.at[g, 2 * m + kv],
        )
        for g in range(GROUPS)
        for m in range(MOST)
        for kv in range(2)
    ]


def pick_rest_kernel(sel_ref, x_ref, o_ref, sems):
    finish(go(picked(sel_ref, x_ref, o_ref, sems, pl.ds(WF, WR))))


def pick_rest(sel, x):
    return pl.pallas_call(
        pick_rest_kernel,
        grid=(1,),
        in_specs=[pl.BlockSpec(memory_space=SMEM), whole(LOCAL_KV)],
        out_specs=pl.BlockSpec(memory_space=ANY),
        out_shape=jax.ShapeDtypeStruct((GROUPS, SEND_REST, WR), BF16),
        scratch_shapes=[pltpu.SemaphoreType.DMA((GROUPS, 2 * MOST))],
        compiler_params=params(),
        cost_estimate=cost(0, (SLOTS + TILES) * 2 * TILE * WR * 2),
        name="pick_rest",
    )(sel, x)


def text_chunk(x_ref, text_ref, which, c, lanes):
    if c < TCHUNKS - 1:
        return x_ref[2 * c : 2 * c + 2, which, :, lanes].reshape(256, HD)
    return text_ref[:, lanes]


def head_lanes(j):
    return pl.ds(pl.multiple_of(j * HD, HD), HD)


def whole(shape):
    return pl.BlockSpec(shape, lambda i: (0,) * len(shape))


TEXT = (TXT, W)
LOCAL_KV = (TILES, 2, TILE, W)


def thirds(x):
    first = x.astype(BF16).astype(F32)
    second = (x - first).astype(BF16).astype(F32)
    return first, second, x - first - second


def put(lane, block, at, column):
    return jnp.where(lane == at, column, block)


def take(lane, block, low, high, j):
    hit = (lane >= low) & (lane < high) & (lane % 8 == j)
    return jnp.sum(jnp.where(hit, block, 0.0), axis=1, keepdims=True)


def send_first_kernel(
    sel_ref, n_ref, tq_ref, tk_ref, tv_ref, x_ref, o_ref, s_ref, part_ref, sems, part_sems
):
    tiles = go(picked(sel_ref, x_ref, o_ref, sems, pl.ds(0, WF)))
    live = lax.broadcasted_iota(jnp.int32, (TXT, TXT), 1) < n_ref[0]
    lane = lax.broadcasted_iota(jnp.int32, (TXT, HD), 1)
    stats = jnp.zeros((TXT, HD), F32)
    for j in range(NH):
        lanes = slice(j * HD, (j + 1) * HD)
        query = tq_ref[:, lanes]
        top = None
        for c in range(TCHUNKS):
            s = dot_nt(query, text_chunk(x_ref, tk_ref, 0, c, lanes)) * FACTOR2
            if c == TCHUNKS - 1:
                s = jnp.where(live, s, NEGATIVE)
            s_ref[c] = s
            top = s if top is None else jnp.maximum(top, s)
        top = jnp.max(top, axis=1, keepdims=True).astype(BF16).astype(F32)
        total, out = None, None
        for c in range(TCHUNKS):
            p = jnp.exp2(s_ref[c] - top)
            part = dot_nn(p.astype(BF16), text_chunk(x_ref, tv_ref, 1, c, lanes))
            total = p if total is None else total + p
            out = part if out is None else out + part
        total = jnp.sum(total, axis=1, keepdims=True)
        part_ref[j] = out.astype(BF16)
        stats = put(lane, stats, j, top)
        for n, third in enumerate(thirds(total)):
            stats = put(lane, stats, 8 * (n + 1) + j, third)
    part_ref[NH] = stats.astype(BF16)
    parts = go(
        [
            pltpu.make_async_copy(
                part_ref.at[n, pl.ds(g * TROWS, TROWS)],
                o_ref.at[g, pl.ds(PAIR_ROWS + n // 2 * TROWS, TROWS), pl.ds(n % 2 * HD, HD)],
                part_sems.at[g, n],
            )
            for g in range(GROUPS)
            for n in range(NH + 1)
        ]
    )
    finish(tiles + parts)


def send_first(sel, n, tq, tk, tv, x):
    return pl.pallas_call(
        send_first_kernel,
        grid=(1,),
        in_specs=[pl.BlockSpec(memory_space=SMEM)] * 2 + [whole(TEXT)] * 3 + [whole(LOCAL_KV)],
        out_specs=pl.BlockSpec(memory_space=ANY),
        out_shape=jax.ShapeDtypeStruct((GROUPS, SEND_FIRST, WF), BF16),
        scratch_shapes=[
            pltpu.VMEM((TCHUNKS, TXT, 256), F32),
            pltpu.VMEM((NH + 1, TXT, HD), BF16),
            pltpu.SemaphoreType.DMA((GROUPS, 2 * MOST)),
            pltpu.SemaphoreType.DMA((GROUPS, NH + 1)),
        ],
        compiler_params=params(),
        cost_estimate=cost(4 * NH * TXT * TCHUNKS * 256 * HD, 5 << 20, NH * TXT * 1280),
        name="send_first",
    )(sel, n, tq, tk, tv, x)


def text_stats_kernel(own_ref, got_ref, tg_ref, in_ref, o_ref, out_ref, parts, stats_ref, sem, sems):
    load = go([pltpu.make_async_copy(got_ref.at[:, pl.ds(PAIR_ROWS, 2 * TROWS)], parts, sem)])
    lane_all = lax.broadcasted_iota(jnp.int32, (TXT, HD), 1)
    lane = lax.broadcasted_iota(jnp.int32, (TROWS, HD), 1)
    mine = pl.ds(pl.multiple_of(own_ref[0] * TROWS, TROWS), TROWS)
    finish(load)
    received = parts[:, TROWS:, HD:].astype(F32).reshape(TXT, HD)
    stats = jnp.zeros((TROWS, HD), F32)
    for j in range(NH):
        lanes = slice(j * HD, (j + 1) * HD)
        tops = take(lane_all, received, 0, 8, j).reshape(GROUPS, TROWS, 1)
        totals = take(lane_all, received, 8, 32, j).reshape(GROUPS, TROWS, 1)
        top = jnp.max(tops, axis=0)
        scale = jnp.exp2(tops - top[None])
        total = jnp.sum(scale * totals, axis=0)
        part = parts[:, j // 2 * TROWS : (j // 2 + 1) * TROWS, j % 2 * HD : (j % 2 + 1) * HD]
        out = jnp.sum(scale * part.astype(F32), axis=0) / total
        out_ref[:, lanes] = out.astype(BF16)
        offset = jnp.sum(tg_ref[mine, lanes].astype(F32) * out, axis=1, keepdims=True)
        for n, third in enumerate(thirds(top + jnp.log2(total)) + thirds(offset)):
            stats = put(lane, stats, 8 * n + j, third)
    stats_ref[...] = stats.astype(BF16)
    finish(
        go(
            [
                pltpu.make_async_copy(
                    stats_ref, o_ref.at[g, pl.ds(PAIR_ROWS, TROWS)], sems.at[g]
                )
                for g in range(GROUPS)
            ]
        )
    )


def text_stats(own, got, tg, send):
    return pl.pallas_call(
        text_stats_kernel,
        grid=(1,),
        in_specs=[pl.BlockSpec(memory_space=SMEM)]
        + any_specs(1)
        + [whole(TEXT)]
        + any_specs(1),
        out_specs=[pl.BlockSpec(memory_space=ANY), whole((TROWS, W))],
        out_shape=[
            jax.ShapeDtypeStruct(send.shape, BF16),
            jax.ShapeDtypeStruct((TROWS, W), BF16),
        ],
        scratch_shapes=[
            pltpu.VMEM((GROUPS, 2 * TROWS, WF), BF16),
            pltpu.VMEM((TROWS, WR), BF16),
            pltpu.SemaphoreType.DMA,
            pltpu.SemaphoreType.DMA((GROUPS,)),
        ],
        input_output_aliases={3: 0},
        compiler_params=params(),
        cost_estimate=cost(TXT * W * 8, 1 << 19),
        name="text_stats",
    )(own, got, tg, send)


def text_backward_kernel(
    n_ref, got_ref, tq_ref, tk_ref, tv_ref, tg_ref, x_ref, tqg_ref, acc_ref, dx_ref, rows, sem
):
    load = go(
        [
            pltpu.make_async_copy(
                got_ref.at[:, pl.ds(PAIR_ROWS, TROWS), pl.ds(0, HD)], rows, sem
            )
        ]
    )
    live = lax.broadcasted_iota(jnp.int32, (TXT, TXT), 1) < n_ref[0]
    lane = lax.broadcasted_iota(jnp.int32, (TXT, HD), 1)
    finish(load)

    def head(j, carry):
        lanes = head_lanes(j)
        stats = rows[...].astype(F32).reshape(TXT, HD)
        log_total = take(lane, stats, 0, 24, j)
        offset = take(lane, stats, 24, 48, j)
        query, grad = tq_ref[:, lanes], tg_ref[:, lanes]
        query_grad = None
        for c in range(TCHUNKS):
            key = text_chunk(x_ref, tk_ref, 0, c, lanes)
            value = text_chunk(x_ref, tv_ref, 1, c, lanes)
            s = dot_nt(query, key) * FACTOR2
            if c == TCHUNKS - 1:
                s = jnp.where(live, s, NEGATIVE)
            p = jnp.exp2(s - log_total)
            ds = (p * (dot_nt(grad, value) - offset)).astype(BF16)
            p = p.astype(BF16)
            part = dot_nn(ds, key)
            query_grad = part if query_grad is None else query_grad + part
            key_grad = dot_tn(ds, query)
            value_grad = dot_tn(p, grad)
            if c < TCHUNKS - 1:
                dx_ref[2 * c : 2 * c + 2, 0, :, lanes] = key_grad.reshape(2, TILE, HD)
                dx_ref[2 * c : 2 * c + 2, 1, :, lanes] = value_grad.reshape(2, TILE, HD)
            else:
                acc_ref[0, :, lanes] = key_grad
                acc_ref[1, :, lanes] = value_grad
        tqg_ref[:, lanes] = query_grad * FACTOR
        return carry

    lax.fori_loop(0, NH, head, 0)


def text_backward(n, got, tq, tk, tv, tg, x):
    return pl.pallas_call(
        text_backward_kernel,
        grid=(1,),
        in_specs=[pl.BlockSpec(memory_space=SMEM)]
        + any_specs(1)
        + [whole(TEXT)] * 4
        + [whole(LOCAL_KV)],
        out_specs=[whole(TEXT), whole((2, TXT, W)), whole(LOCAL_KV)],
        out_shape=[
            jax.ShapeDtypeStruct(TEXT, F32),
            jax.ShapeDtypeStruct((2, TXT, W), F32),
            jax.ShapeDtypeStruct(LOCAL_KV, F32),
        ],
        scratch_shapes=[
            pltpu.VMEM((GROUPS, TROWS, HD), BF16),
            pltpu.SemaphoreType.DMA,
        ],
        compiler_params=params(),
        cost_estimate=cost(10 * NH * TXT * TCHUNKS * 256 * HD, 8 << 20, NH * TXT * 1280),
        name="text_backward",
    )(n, got, tq, tk, tv, tg, x)


CHUNKS = KT // 2 + 1


def video_kernel(first, slot_ref, count_ref, n_ref, kv_ref, qg_ref, got_ref, tk_ref, tv_ref, *refs):
    if first:
        out_ref, back_ref, own_ref, text_ref = refs[:4]
        refs = refs[4:]
    else:
        tqg_ref, tacc_ref, text0_ref, out_ref, back_ref, own_ref = refs[:6]
        refs = refs[6:]
    keys, values, s_ref, p_ref, dk_acc, dv_acc, tk_acc, tv_acc, pool = refs
    pool[:TILES] = kv_ref[...]
    pool[TILES:] = got_ref[...].reshape(SLOTS, 2, TILE, HD)
    keys[0] = tk_ref[...]
    values[0] = tv_ref[...]
    dk_acc[...] = jnp.zeros((POOL, TILE, HD), F32)
    dv_acc[...] = jnp.zeros((POOL, TILE, HD), F32)
    if first:
        tk_acc[...] = jnp.zeros((TXT, HD), F32)
        tv_acc[...] = jnp.zeros((TXT, HD), F32)
    else:
        tk_acc[...] = tacc_ref[0, :, WF:]
        tv_acc[...] = tacc_ref[1, :, WF:]
    text_live = lax.broadcasted_iota(jnp.int32, (TXT, TILE), 0) < n_ref[0]

    def tile(i, carry):
        count = count_ref[i]
        query, grad = qg_ref[i, 0], qg_ref[i, 1]

        def run(pairs):
            slots = [slot_ref[i * KT + e] for e in range(2 * pairs)]
            for e in range(2 * pairs):
                half = pl.ds((e % 2) * TILE, TILE)
                keys[1 + e // 2, half] = pool[slots[e], 0]
                values[1 + e // 2, half] = pool[slots[e], 1]
            top = None
            for c in range(pairs + 1):
                s = dot_nt(keys[c], query) * FACTOR2
                if c == 0:
                    s = jnp.where(text_live, s, NEGATIVE)
                elif c == pairs:
                    s = jnp.concatenate(
                        [s[:TILE], jnp.where(2 * pairs <= count, s[TILE:], NEGATIVE)], axis=0
                    )
                s_ref[c] = s
                part = jnp.max(s.reshape(32, 8, TILE), axis=0)
                top = part if top is None else jnp.maximum(top, part)
            top = jnp.max(top, axis=0, keepdims=True)
            total = None
            for c in range(pairs + 1):
                p = jnp.exp2(s_ref[c] - top)
                s_ref[c] = p
                part = jnp.sum(p.reshape(32, 8, TILE), axis=0)
                total = part if total is None else total + part
            scale = 1.0 / jnp.sum(total, axis=0, keepdims=True)
            out = None
            for c in range(pairs + 1):
                p = s_ref[c] * scale
                s_ref[c] = p
                p = p.astype(BF16)
                p_ref[c] = p
                part = dot_tn(p, values[c])
                out = part if out is None else out + part
            out_ref[i, 0] = out.astype(BF16)
            offset = jnp.sum((grad.astype(F32) * out).T, axis=0, keepdims=True)
            query_grad = None
            for c in range(pairs + 1):
                ds = (s_ref[c] * (dot_nt(values[c], grad) - offset)).astype(BF16)
                part = dot_tn(ds, keys[c])
                query_grad = part if query_grad is None else query_grad + part
                key_grad = dot_nn(ds, query)
                value_grad = dot_nn(p_ref[c], grad)
                if c == 0:
                    tk_acc[...] += key_grad
                    tv_acc[...] += value_grad
                else:
                    for e in (0, 1):
                        slot = slots[2 * (c - 1) + e]
                        dk_acc[slot] += key_grad[e * TILE : (e + 1) * TILE]
                        dv_acc[slot] += value_grad[e * TILE : (e + 1) * TILE]
            out_ref[i, 1] = (query_grad * FACTOR).astype(BF16)

        for pairs in range(1, KT // 2 + 1):

            @pl.when((count + 1) // 2 == pairs)
            def _():
                run(pairs)

        return carry

    lax.fori_loop(0, TILES, tile, 0)

    own_ref[:, 0] = dk_acc[:TILES]
    own_ref[:, 1] = dv_acc[:TILES]
    for g in range(GROUPS):
        for m in range(MOST):
            slot = TILES + g * MOST + m
            back_ref[g, 2 * m * TILE : (2 * m + 1) * TILE] = (dk_acc[slot] * FACTOR).astype(BF16)
            back_ref[g, (2 * m + 1) * TILE : (2 * m + 2) * TILE] = dv_acc[slot].astype(BF16)
    if first:
        text_ref[0] = tk_acc[...]
        text_ref[1] = tv_acc[...]
        return

    def store(n, values):
        at = PAIR_ROWS + n * TROWS
        back_ref[:, at : at + TROWS] = values.reshape(GROUPS, TROWS, HD).astype(BF16)

    for h in range(NH):
        lanes = slice(h * HD, (h + 1) * HD)
        if h < NF:
            key_grad = tacc_ref[0, :, lanes] + text0_ref[0, :, lanes]
            value_grad = tacc_ref[1, :, lanes] + text0_ref[1, :, lanes]
        else:
            key_grad, value_grad = tk_acc[...], tv_acc[...]
        store(h, tqg_ref[:, lanes])
        store(NH + h, key_grad * FACTOR)
        store(2 * NH + h, value_grad)


def video(first, slot, count, n, x, got, tk, tv, *text):
    base, heads = (0, NF) if first else (NF, NH - NF)
    rows = PAIR_ROWS if first else BACK_REST
    width = heads * HD
    smem = pl.BlockSpec(memory_space=SMEM)
    per_head = pl.BlockSpec((TXT, HD), lambda j: (0, base + j))
    pair = (TILES, 2, TILE, HD)
    in_specs = [
        smem,
        smem,
        smem,
        pl.BlockSpec(pair, lambda j: (0, 0, 0, base + j)),
        pl.BlockSpec(pair, lambda j: (0, 1, 0, base + j)),
        pl.BlockSpec((GROUPS, PAIR_ROWS, HD), lambda j: (0, 0, j)),
        per_head,
        per_head,
    ]
    out_specs = [
        pl.BlockSpec(pair, lambda j: (0, 0, 0, j)),
        pl.BlockSpec((GROUPS, rows, HD), lambda j: (0, 0, j)),
        pl.BlockSpec(pair, lambda j: (0, 0, 0, j)),
    ]
    out_shape = [
        jax.ShapeDtypeStruct((TILES, 2, TILE, width), BF16),
        jax.ShapeDtypeStruct((GROUPS, rows, width), BF16),
        jax.ShapeDtypeStruct((TILES, 2, TILE, width), F32),
    ]
    if first:
        out_specs.append(pl.BlockSpec((2, TXT, HD), lambda j: (0, 0, j)))
        out_shape.append(jax.ShapeDtypeStruct((2, TXT, WF), F32))
    else:
        in_specs += [whole(TEXT), whole((2, TXT, W)), whole((2, TXT, WF))]
    return pl.pallas_call(
        functools.partial(video_kernel, first),
        grid=(heads,),
        in_specs=in_specs,
        out_specs=out_specs,
        out_shape=out_shape,
        scratch_shapes=[
            pltpu.VMEM((CHUNKS, 256, HD), BF16),
            pltpu.VMEM((CHUNKS, 256, HD), BF16),
            pltpu.VMEM((CHUNKS, 256, TILE), F32),
            pltpu.VMEM((CHUNKS, 256, TILE), BF16),
            pltpu.VMEM((POOL, TILE, HD), F32),
            pltpu.VMEM((POOL, TILE, HD), F32),
            pltpu.VMEM((TXT, HD), F32),
            pltpu.VMEM((TXT, HD), F32),
            pltpu.VMEM((POOL, 2, TILE, HD), BF16),
        ],
        compiler_params=params(),
        cost_estimate=cost(
            12 * heads * TLOCAL * 1280 * HD, heads * (8 << 20), heads * TLOCAL * 1280
        ),
        name="video_first" if first else "video_rest",
    )(slot, count, n, x, x, got, tk, tv, *text)


def combine_kernel(sel_ref, back_ref, own_ref, dx_ref, half_ref, *refs):
    out_ref, acc = refs[-2:]
    acc[:, 0] = (own_ref[:, 0] + dx_ref[:, 0]) * FACTOR
    acc[:, 1] = own_ref[:, 1] + dx_ref[:, 1]

    def add(g, carry):
        for m in range(MOST):
            at = sel_ref[g * MOST + m]
            part = back_ref[g, 2 * m * TILE : 2 * (m + 1) * TILE].astype(F32)
            acc[at] += part.reshape(2, TILE, HD)
        return carry

    lax.fori_loop(0, GROUPS, add, 0)
    out_ref[:, :2] = half_ref[...]
    out_ref[:, 2:] = acc[...].astype(BF16)


def combine(first, sel, back, own, dx, half, *packed):
    base, heads = (0, NF) if first else (NF, NH - NF)
    pair = (TILES, 2, TILE, HD)
    return pl.pallas_call(
        combine_kernel,
        grid=(heads,),
        in_specs=[
            pl.BlockSpec(memory_space=SMEM),
            pl.BlockSpec((GROUPS, PAIR_ROWS, HD), lambda j: (0, 0, j)),
            pl.BlockSpec(pair, lambda j: (0, 0, 0, j)),
            pl.BlockSpec(pair, lambda j: (0, 0, 0, base + j)),
            pl.BlockSpec(pair, lambda j: (0, 0, 0, j)),
        ]
        + any_specs(len(packed)),
        out_specs=pl.BlockSpec((TILES, 4, TILE, HD), lambda j: (0, 0, 0, base + j)),
        out_shape=jax.ShapeDtypeStruct((TILES, 4, TILE, W), BF16),
        scratch_shapes=[pltpu.VMEM(pair, F32)],
        input_output_aliases={5: 0} if packed else {},
        compiler_params=params(),
        cost_estimate=cost(heads * TLOCAL * HD * 64, heads * (5 << 20)),
        name="combine_first" if first else "combine_rest",
    )(sel, back, own, dx, half, *packed)


def text_sum_kernel(back_ref, out_ref, o_ref, rows, sem):
    load = [pltpu.make_async_copy(back_ref.at[:, pl.ds(PAIR_ROWS, 3 * NH * TROWS)], rows, sem)]
    finish(go(load))
    total = jnp.sum(rows[...].astype(F32), axis=0).astype(BF16)
    o_ref[0] = out_ref[...]
    for n in range(3 * NH):
        h = n % NH
        o_ref[n // NH + 1, :, h * HD : (h + 1) * HD] = total[n * TROWS : (n + 1) * TROWS]


def text_sum(back, out):
    return pl.pallas_call(
        text_sum_kernel,
        grid=(1,),
        in_specs=any_specs(1) + [whole((TROWS, W))],
        out_specs=whole((4, TROWS, W)),
        out_shape=jax.ShapeDtypeStruct((4, TROWS, W), BF16),
        scratch_shapes=[
            pltpu.VMEM((GROUPS, 3 * NH * TROWS, WR), BF16),
            pltpu.SemaphoreType.DMA,
        ],
        compiler_params=params(),
        cost_estimate=cost(GROUPS * 9 * TROWS * WR, 1 << 20),
        name="text_sum",
    )(back, out)


STEPS = ((1, 1), (2, 2), (4, 6), (8, 8))


def swapped(x, mask):
    return lax.ppermute(x, "seq", [(i, i ^ mask) for i in range(GROUPS)])


def tables(tile_list, tile_count, own):
    live = jnp.arange(KT)[None, :] < tile_count[:, None]
    listed = jnp.where(live, tile_list, -1)

    def ranked(wanted):
        before = jnp.arange(TILES)[:, None] < jnp.arange(TILES)[None, :]
        return jnp.sum(jnp.where(before[None], wanted[:, :, None], 0), axis=1)

    mine = own * TILES + jnp.arange(TILES)
    asked = jnp.any(
        listed.reshape(GROUPS, TILES * KT, 1) == mine[None, None, :], axis=1
    ).astype(jnp.int32)
    rank = ranked(asked)
    chosen = (asked[:, None, :] > 0) & (rank[:, None, :] == jnp.arange(MOST)[None, :, None])
    sel = jnp.sum(jnp.where(chosen, jnp.arange(TILES)[None, None, :], 0), axis=2).reshape(SLOTS)

    my_list = lax.dynamic_slice_in_dim(listed, own * TILES, TILES, 0).reshape(TILES * KT)
    hits = my_list[:, None] == jnp.arange(GROUPS * TILES)[None, :]
    needed = jnp.any(hits, axis=0).astype(jnp.int32).reshape(GROUPS, TILES)
    where_to = TILES + jnp.arange(GROUPS)[:, None] * MOST + jnp.minimum(ranked(needed), MOST - 1)
    local = jnp.arange(GROUPS)[:, None] == own
    where_to = jnp.where(local, jnp.arange(TILES)[None, :], where_to).reshape(GROUPS * TILES)
    slot = jnp.sum(jnp.where(hits, where_to[None, :], 0), axis=1)
    count = lax.dynamic_slice_in_dim(tile_count, own * TILES, TILES, 0)
    return sel.astype(jnp.int32), slot.astype(jnp.int32), count.astype(jnp.int32)


def body(
    video_query,
    video_key,
    video_value,
    video_grad,
    text_query,
    text_key,
    text_value,
    text_grad,
    tile_list,
    tile_count,
    text_mask,
):
    own = lax.axis_index("seq")
    x = lax.all_to_all(
        pack(video_key, video_value, video_query, video_grad), "head", 0, 0, tiled=True
    )
    sel, slot, count = tables(tile_list, tile_count, own)
    n = jnp.sum((text_mask > 0).astype(jnp.int32)).reshape(1)
    n_own = jnp.where(own == 0, n, 0)
    text = (text_query, text_key, text_value)

    send = send_first(sel, n_own, *text, x)
    got0 = lax.all_to_all(send, "seq", 0, 0, tiled=True)
    send, text_out = text_stats(own.reshape(1), got0, text_grad, pick_rest(sel, x))
    got = lax.all_to_all(send, "seq", 0, 0, tiled=True)
    half0, back0, own0, text0 = video(
        True, slot, count, n, x, got0, text_key, text_value
    )
    back0 = lax.all_to_all(back0, "seq", 0, 0, tiled=True)
    tqg, tacc, dx = text_backward(n_own, got, *text, text_grad, x)
    half, back, own_grads = video(
        False, slot, count, n, x, got, text_key, text_value, tqg, tacc, text0
    )
    back = lax.all_to_all(back, "seq", 0, 0, tiled=True)
    packed = combine(True, sel, back0, own0, dx, half0)
    packed = combine(False, sel, back, own_grads, dx, half, packed)

    gathered = text_sum(back, text_out)[None]
    for bit, mask in STEPS:
        theirs = swapped(gathered, mask)
        first = jnp.concatenate([gathered, theirs], axis=0)
        second = jnp.concatenate([theirs, gathered], axis=0)
        gathered = jnp.where((own & bit) == 0, first, second)
    text_rows = jnp.transpose(gathered, (1, 0, 2, 3)).reshape(4, TXT, W)

    attended_video, video_query_grad, video_key_grad, video_value_grad = unpack(
        lax.all_to_all(packed, "head", 0, 0, tiled=True)
    )
    return (
        attended_video,
        video_query_grad,
        video_key_grad,
        video_value_grad,
        text_rows[0],
        text_rows[1],
        text_rows[2],
        text_rows[3],
    )


def solution(mesh):
    tokens, heads = P(("seq", "head"), None), P(None, "head")
    return jax.shard_map(
        body,
        mesh=mesh,
        in_specs=(tokens,) * 4 + (heads,) * 4 + (P(),) * 3,
        out_specs=(tokens,) * 4 + (heads,) * 4,
        check_vma=False,
    )
```

```python
import functools

import jax
import jax.numpy as jnp
from jax import lax
from jax.experimental import pallas as pl
from jax.experimental.pallas import tpu as pltpu
from jax.sharding import PartitionSpec as P

HD = 128
TXT = 256
TILE = 128
KT = 8
MOST = 2
GROUPS = 16
HEADS = 8
TILES = 8
NH = 3
W = NH * HD
SLOTS = GROUPS * MOST
POOL = TILES + SLOTS
TROWS = TXT // GROUPS
TLOCAL = TILES * TILE
TCHUNKS = TLOCAL // 256 + 1
PAIR_ROWS = MOST * 2 * TILE
SEND_FIRST = PAIR_ROWS + 2 * TROWS
SEND_REST = PAIR_ROWS + TROWS
BACK_REST = PAIR_ROWS + 3 * NH * TROWS
NF = 2
WF = NF * HD
WR = W - WF

NEGATIVE = -1e30
FACTOR = HD**-0.5
LOG2E = 1.4426950408889634
FACTOR2 = FACTOR * LOG2E
VMEM_LIMIT = 67043328

F32 = jnp.float32
BF16 = jnp.bfloat16
SMEM = pltpu.SMEM
ANY = pl.ANY


def dot_nt(a, b):
    return lax.dot_general(a, b, (((1,), (1,)), ((), ())), preferred_element_type=F32)


def dot_nn(a, b):
    return lax.dot_general(a, b, (((1,), (0,)), ((), ())), preferred_element_type=F32)


def dot_tn(a, b):
    return lax.dot_general(a, b, (((0,), (0,)), ((), ())), preferred_element_type=F32)


def params(**kw):
    return pltpu.CompilerParams(vmem_limit_bytes=VMEM_LIMIT, **kw)


def cost(flops, nbytes, exps=0):
    return pl.CostEstimate(
        flops=int(flops), bytes_accessed=int(nbytes), transcendentals=int(exps)
    )


def go(copies):
    for copy in copies:
        copy.start()
    return copies


def finish(copies):
    for copy in copies:
        copy.wait()


def columns(h):
    return pl.ds(h * W, W)


def pack_kernel(k_ref, v_ref, q_ref, g_ref, o_ref, rows, in_sems, out_sems):
    refs = (k_ref, v_ref, q_ref, g_ref)
    loads = go([pltpu.make_async_copy(refs[n], rows.at[n], in_sems.at[n]) for n in range(4)])
    stores = []
    for n in range(4):
        loads[n].wait()
        stores += go(
            [
                pltpu.make_async_copy(
                    rows.at[n, :, columns(h)], o_ref.at[h, n], out_sems.at[n, h]
                )
                for h in range(HEADS)
            ]
        )
    finish(stores)


def any_specs(n):
    return [pl.BlockSpec(memory_space=ANY)] * n


def pack(k, v, q, g):
    return pl.pallas_call(
        pack_kernel,
        in_specs=any_specs(4),
        out_specs=pl.BlockSpec(memory_space=ANY),
        out_shape=jax.ShapeDtypeStruct((HEADS, 4, TILE, W), BF16),
        scratch_shapes=[
            pltpu.VMEM((4, TILE, HEADS * W), BF16),
            pltpu.SemaphoreType.DMA((4,)),
            pltpu.SemaphoreType.DMA((4, HEADS)),
        ],
        compiler_params=params(),
        cost_estimate=cost(0, 8 * TILE * HEADS * W * 2),
        name="pack",
    )(k, v, q, g)


def unpack_kernel(x_ref, a_ref, b_ref, c_ref, d_ref, rows, in_sems, out_sems):
    refs = (a_ref, b_ref, c_ref, d_ref)
    loads = [
        go(
            [
                pltpu.make_async_copy(
                    x_ref.at[h, n], rows.at[n, :, columns(h)], in_sems.at[n, h]
                )
                for h in range(HEADS)
            ]
        )
        for n in range(4)
    ]
    stores = []
    for n in range(4):
        finish(loads[n])
        stores += go([pltpu.make_async_copy(rows.at[n], refs[n], out_sems.at[n])])
    finish(stores)


def unpack(x):
    return pl.pallas_call(
        unpack_kernel,
        in_specs=any_specs(1),
        out_specs=any_specs(4),
        out_shape=[jax.ShapeDtypeStruct((TILE, HEADS * W), BF16)] * 4,
        scratch_shapes=[
            pltpu.VMEM((4, TILE, HEADS * W), BF16),
            pltpu.SemaphoreType.DMA((4, HEADS)),
            pltpu.SemaphoreType.DMA((4,)),
        ],
        compiler_params=params(),
        cost_estimate=cost(0, 8 * TILE * HEADS * W * 2),
        name="unpack",
    )(x)


def picked(sel_ref, x_ref, o_ref, sems, lanes):
    return [
        pltpu.make_async_copy(
            x_ref.at[sel_ref[g * MOST + m], kv, :, lanes],
            o_ref.at[g, pl.ds((2 * m + kv) * TILE, TILE)],
            sems.at[g, 2 * m + kv],
        )
        for g in range(GROUPS)
        for m in range(MOST)
        for kv in range(2)
    ]


def text_chunk(x_ref, text_ref, which, c, lanes):
    if c < TCHUNKS - 1:
        return x_ref[2 * c : 2 * c + 2, which, :, lanes].reshape(256, HD)
    return text_ref[:, lanes]


def head_lanes(j):
    return pl.ds(pl.multiple_of(j * HD, HD), HD)


def whole(shape):
    return pl.BlockSpec(shape, lambda i: (0,) * len(shape))


TEXT = (TXT, W)
LOCAL_KV = (TILES, 2, TILE, W)


def thirds(x):
    first = x.astype(BF16).astype(F32)
    second = (x - first).astype(BF16).astype(F32)
    return first, second, x - first - second


def put(lane, block, at, column):
    return jnp.where(lane == at, column, block)


def take(lane, block, low, high, j):
    hit = (lane >= low) & (lane < high) & (lane % 8 == j)
    return jnp.sum(jnp.where(hit, block, 0.0), axis=1, keepdims=True)


def send_kernel(
    sel_ref,
    n_ref,
    tq_ref,
    tk_ref,
    tv_ref,
    x_ref,
    o_ref,
    rest_ref,
    s_ref,
    part_ref,
    sems,
    rest_sems,
    part_sems,
):
    tiles = go(picked(sel_ref, x_ref, o_ref, sems, pl.ds(0, WF)))
    tiles += go(picked(sel_ref, x_ref, rest_ref, rest_sems, pl.ds(WF, WR)))
    live = lax.broadcasted_iota(jnp.int32, (TXT, TXT), 1) < n_ref[0]
    lane = lax.broadcasted_iota(jnp.int32, (TXT, HD), 1)
    stats = jnp.zeros((TXT, HD), F32)
    for j in range(NH):
        lanes = slice(j * HD, (j + 1) * HD)
        query = tq_ref[:, lanes]
        top = None
        for c in range(TCHUNKS):
            s = dot_nt(query, text_chunk(x_ref, tk_ref, 0, c, lanes)) * FACTOR2
            if c == TCHUNKS - 1:
                s = jnp.where(live, s, NEGATIVE)
            s_ref[c] = s
            top = s if top is None else jnp.maximum(top, s)
        top = jnp.max(top, axis=1, keepdims=True).astype(BF16).astype(F32)
        total, out = None, None
        for c in range(TCHUNKS):
            p = jnp.exp2(s_ref[c] - top)
            part = dot_nn(p.astype(BF16), text_chunk(x_ref, tv_ref, 1, c, lanes))
            total = p if total is None else total + p
            out = part if out is None else out + part
        total = jnp.sum(total, axis=1, keepdims=True)
        part_ref[j] = out.astype(BF16)
        stats = put(lane, stats, j, top)
        for n, third in enumerate(thirds(total)):
            stats = put(lane, stats, 8 * (n + 1) + j, third)
    part_ref[NH] = stats.astype(BF16)
    parts = go(
        [
            pltpu.make_async_copy(
                part_ref.at[n, pl.ds(g * TROWS, TROWS)],
                o_ref.at[g, pl.ds(PAIR_ROWS + n // 2 * TROWS, TROWS), pl.ds(n % 2 * HD, HD)],
                part_sems.at[g, n],
            )
            for g in range(GROUPS)
            for n in range(NH + 1)
        ]
    )
    finish(tiles + parts)


def send(sel, n, tq, tk, tv, x):
    return pl.pallas_call(
        send_kernel,
        grid=(1,),
        in_specs=[pl.BlockSpec(memory_space=SMEM)] * 2 + [whole(TEXT)] * 3 + [whole(LOCAL_KV)],
        out_specs=any_specs(2),
        out_shape=[
            jax.ShapeDtypeStruct((GROUPS, SEND_FIRST, WF), BF16),
            jax.ShapeDtypeStruct((GROUPS, SEND_REST, WR), BF16),
        ],
        scratch_shapes=[
            pltpu.VMEM((TCHUNKS, TXT, 256), F32),
            pltpu.VMEM((NH + 1, TXT, HD), BF16),
            pltpu.SemaphoreType.DMA((GROUPS, 2 * MOST)),
            pltpu.SemaphoreType.DMA((GROUPS, 2 * MOST)),
            pltpu.SemaphoreType.DMA((GROUPS, NH + 1)),
        ],
        compiler_params=params(),
        cost_estimate=cost(4 * NH * TXT * TCHUNKS * 256 * HD, 5 << 20, NH * TXT * 1280),
        name="send",
    )(sel, n, tq, tk, tv, x)


def text_stats_kernel(own_ref, got_ref, tg_ref, in_ref, o_ref, out_ref, parts, stats_ref, sem, sems):
    load = go([pltpu.make_async_copy(got_ref.at[:, pl.ds(PAIR_ROWS, 2 * TROWS)], parts, sem)])
    lane_all = lax.broadcasted_iota(jnp.int32, (TXT, HD), 1)
    lane = lax.broadcasted_iota(jnp.int32, (TROWS, HD), 1)
    mine = pl.ds(pl.multiple_of(own_ref[0] * TROWS, TROWS), TROWS)
    finish(load)
    received = parts[:, TROWS:, HD:].astype(F32).reshape(TXT, HD)
    stats = jnp.zeros((TROWS, HD), F32)
    for j in range(NH):
        lanes = slice(j * HD, (j + 1) * HD)
        tops = take(lane_all, received, 0, 8, j).reshape(GROUPS, TROWS, 1)
        totals = take(lane_all, received, 8, 32, j).reshape(GROUPS, TROWS, 1)
        top = jnp.max(tops, axis=0)
        scale = jnp.exp2(tops - top[None])
        total = jnp.sum(scale * totals, axis=0)
        part = parts[:, j // 2 * TROWS : (j // 2 + 1) * TROWS, j % 2 * HD : (j % 2 + 1) * HD]
        out = jnp.sum(scale * part.astype(F32), axis=0) / total
        out_ref[:, lanes] = out.astype(BF16)
        offset = jnp.sum(tg_ref[mine, lanes].astype(F32) * out, axis=1, keepdims=True)
        for n, third in enumerate(thirds(top + jnp.log2(total)) + thirds(offset)):
            stats = put(lane, stats, 8 * n + j, third)
    stats_ref[...] = stats.astype(BF16)
    finish(
        go(
            [
                pltpu.make_async_copy(
                    stats_ref, o_ref.at[g, pl.ds(PAIR_ROWS, TROWS)], sems.at[g]
                )
                for g in range(GROUPS)
            ]
        )
    )


def text_stats(own, got, tg, send):
    return pl.pallas_call(
        text_stats_kernel,
        grid=(1,),
        in_specs=[pl.BlockSpec(memory_space=SMEM)]
        + any_specs(1)
        + [whole(TEXT)]
        + any_specs(1),
        out_specs=[pl.BlockSpec(memory_space=ANY), whole((TROWS, W))],
        out_shape=[
            jax.ShapeDtypeStruct(send.shape, BF16),
            jax.ShapeDtypeStruct((TROWS, W), BF16),
        ],
        scratch_shapes=[
            pltpu.VMEM((GROUPS, 2 * TROWS, WF), BF16),
            pltpu.VMEM((TROWS, WR), BF16),
            pltpu.SemaphoreType.DMA,
            pltpu.SemaphoreType.DMA((GROUPS,)),
        ],
        input_output_aliases={3: 0},
        compiler_params=params(),
        cost_estimate=cost(TXT * W * 8, 1 << 19),
        name="text_stats",
    )(own, got, tg, send)


def text_backward_kernel(
    n_ref, got_ref, tq_ref, tk_ref, tv_ref, tg_ref, x_ref, tqg_ref, acc_ref, dx_ref, rows, sem
):
    load = go(
        [
            pltpu.make_async_copy(
                got_ref.at[:, pl.ds(PAIR_ROWS, TROWS), pl.ds(0, HD)], rows, sem
            )
        ]
    )
    live = lax.broadcasted_iota(jnp.int32, (TXT, TXT), 1) < n_ref[0]
    lane = lax.broadcasted_iota(jnp.int32, (TXT, HD), 1)
    finish(load)

    def head(j, carry):
        lanes = head_lanes(j)
        stats = rows[...].astype(F32).reshape(TXT, HD)
        log_total = take(lane, stats, 0, 24, j)
        offset = take(lane, stats, 24, 48, j)
        query, grad = tq_ref[:, lanes], tg_ref[:, lanes]
        query_grad = None
        for c in range(TCHUNKS):
            key = text_chunk(x_ref, tk_ref, 0, c, lanes)
            value = text_chunk(x_ref, tv_ref, 1, c, lanes)
            s = dot_nt(query, key) * FACTOR2
            if c == TCHUNKS - 1:
                s = jnp.where(live, s, NEGATIVE)
            p = jnp.exp2(s - log_total)
            ds = (p * (dot_nt(grad, value) - offset)).astype(BF16)
            p = p.astype(BF16)
            part = dot_nn(ds, key)
            query_grad = part if query_grad is None else query_grad + part
            key_grad = dot_tn(ds, query)
            value_grad = dot_tn(p, grad)
            if c < TCHUNKS - 1:
                dx_ref[2 * c : 2 * c + 2, 0, :, lanes] = key_grad.reshape(2, TILE, HD)
                dx_ref[2 * c : 2 * c + 2, 1, :, lanes] = value_grad.reshape(2, TILE, HD)
            else:
                acc_ref[0, :, lanes] = key_grad
                acc_ref[1, :, lanes] = value_grad
        tqg_ref[:, lanes] = query_grad * FACTOR
        return carry

    lax.fori_loop(0, NH, head, 0)


def text_backward(n, got, tq, tk, tv, tg, x):
    return pl.pallas_call(
        text_backward_kernel,
        grid=(1,),
        in_specs=[pl.BlockSpec(memory_space=SMEM)]
        + any_specs(1)
        + [whole(TEXT)] * 4
        + [whole(LOCAL_KV)],
        out_specs=[whole(TEXT), whole((2, TXT, W)), whole(LOCAL_KV)],
        out_shape=[
            jax.ShapeDtypeStruct(TEXT, F32),
            jax.ShapeDtypeStruct((2, TXT, W), F32),
            jax.ShapeDtypeStruct(LOCAL_KV, F32),
        ],
        scratch_shapes=[
            pltpu.VMEM((GROUPS, TROWS, HD), BF16),
            pltpu.SemaphoreType.DMA,
        ],
        compiler_params=params(),
        cost_estimate=cost(10 * NH * TXT * TCHUNKS * 256 * HD, 8 << 20, NH * TXT * 1280),
        name="text_backward",
    )(n, got, tq, tk, tv, tg, x)


CHUNKS = KT // 2 + 1


def video_kernel(
    first, slot_ref, count_ref, n_ref, x_ref, got_ref, tk_ref, tv_ref, *refs
):
    if first:
        out_ref, back_ref, own_ref, text_ref = refs[:4]
        refs = refs[4:]
    else:
        tqg_ref, tacc_ref, text0_ref, out_ref, back_ref, own_ref = refs[:6]
        refs = refs[6:]
    keys, values, s_ref, p_ref, dk_acc, dv_acc, tk_acc, tv_acc, pool, qg, stage = refs[:11]
    kv_sems, got_sems, qg_sem, back_sems, own_sems = refs[11:]
    base, heads = (0, NF) if first else (NF, NH - NF)
    mine = slice(base * HD, (base + heads) * HD)
    lanes = pl.ds(base * HD, heads * HD)

    def pool_rows(slot, kv):
        return pl.ds(pl.multiple_of((2 * slot + kv) * TILE, TILE), TILE)

    loads = [
        pltpu.make_async_copy(
            x_ref.at[t, kv, :, lanes], pool.at[pool_rows(t, kv)], kv_sems.at[t, kv]
        )
        for t in range(TILES)
        for kv in range(2)
    ]
    loads.append(pltpu.make_async_copy(x_ref.at[:, pl.ds(2, 2), :, lanes], qg, qg_sem))
    loads += [
        pltpu.make_async_copy(
            got_ref.at[g, pl.ds(0, PAIR_ROWS)],
            pool.at[pl.ds(2 * TILES * TILE + g * PAIR_ROWS, PAIR_ROWS)],
            got_sems.at[g],
        )
        for g in range(GROUPS)
    ]
    go(loads)
    keys[0] = tk_ref[:, mine]
    values[0] = tv_ref[:, mine]

    def clear(slot, carry):
        dk_acc[slot] = jnp.zeros((TILE, heads * HD), F32)
        dv_acc[slot] = jnp.zeros((TILE, heads * HD), F32)
        return carry

    lax.fori_loop(0, POOL, clear, 0)
    if first:
        tk_acc[...] = jnp.zeros((TXT, heads * HD), F32)
        tv_acc[...] = jnp.zeros((TXT, heads * HD), F32)
    else:
        tk_acc[...] = tacc_ref[0, :, mine]
        tv_acc[...] = tacc_ref[1, :, mine]
    text_live = lax.broadcasted_iota(jnp.int32, (TXT, TILE), 0) < n_ref[0]
    finish(loads)
    cuts = [slice(h * HD, (h + 1) * HD) for h in range(heads)]

    def tile(i, carry):
        count = count_ref[i]

        def run(pairs):
            slots = [slot_ref[i * KT + e] for e in range(2 * pairs)]
            for e in range(2 * pairs):
                half = pl.ds((e % 2) * TILE, TILE)
                keys[1 + e // 2, half] = pool[pool_rows(slots[e], 0)]
                values[1 + e // 2, half] = pool[pool_rows(slots[e], 1)]
            query = [qg[i, 0, :, cut] for cut in cuts]
            grad = [qg[i, 1, :, cut] for cut in cuts]
            tops, scales, offsets = [], [], []
            for h, cut in enumerate(cuts):
                top = None
                for c in range(pairs + 1):
                    s = dot_nt(keys[c, :, cut], query[h]) * FACTOR2
                    if c == 0:
                        s = jnp.where(text_live, s, NEGATIVE)
                    elif c == pairs:
                        dead = jnp.where(2 * pairs <= count, s[TILE:], NEGATIVE)
                        s = jnp.concatenate([s[:TILE], dead], axis=0)
                    s_ref[h, c] = s
                    part = jnp.max(s.reshape(32, 8, TILE), axis=0)
                    top = part if top is None else jnp.maximum(top, part)
                tops.append(jnp.max(top, axis=0, keepdims=True))
            for h, cut in enumerate(cuts):
                total = None
                for c in range(pairs + 1):
                    p = jnp.exp2(s_ref[h, c] - tops[h])
                    s_ref[h, c] = p
                    part = jnp.sum(p.reshape(32, 8, TILE), axis=0)
                    total = part if total is None else total + part
                scales.append(1.0 / jnp.sum(total, axis=0, keepdims=True))
            for h, cut in enumerate(cuts):
                out = None
                for c in range(pairs + 1):
                    p = s_ref[h, c] * scales[h]
                    s_ref[h, c] = p
                    p = p.astype(BF16)
                    p_ref[h, c] = p
                    part = dot_tn(p, values[c, :, cut])
                    out = part if out is None else out + part
                out_ref[i, 0, :, cut] = out.astype(BF16)
                offsets.append(
                    jnp.sum((grad[h].astype(F32) * out).T, axis=0, keepdims=True)
                )
            for h, cut in enumerate(cuts):
                query_grad = None
                for c in range(pairs + 1):
                    dp = dot_nt(values[c, :, cut], grad[h])
                    ds = (s_ref[h, c] * (dp - offsets[h])).astype(BF16)
                    part = dot_tn(ds, keys[c, :, cut])
                    query_grad = part if query_grad is None else query_grad + part
                    key_grad = dot_nn(ds, query[h])
                    value_grad = dot_nn(p_ref[h, c], grad[h])
                    if c == 0:
                        tk_acc[:, cut] += key_grad
                        tv_acc[:, cut] += value_grad
                    else:
                        for e in (0, 1):
                            slot = slots[2 * (c - 1) + e]
                            rows = slice(e * TILE, (e + 1) * TILE)
                            dk_acc[slot, :, cut] += key_grad[rows]
                            dv_acc[slot, :, cut] += value_grad[rows]
                out_ref[i, 1, :, cut] = (query_grad * FACTOR).astype(BF16)

        for pairs in range(1, KT // 2 + 1):

            @pl.when((count + 1) // 2 == pairs)
            def _():
                run(pairs)

        return carry

    lax.fori_loop(0, TILES, tile, 0)

    stores = go(
        [
            pltpu.make_async_copy(acc.at[pl.ds(0, TILES)], own_ref.at[:, n], own_sems.at[n])
            for n, acc in enumerate((dk_acc, dv_acc))
        ]
    )
    if first:
        text_ref[0] = tk_acc[...]
        text_ref[1] = tv_acc[...]
    else:

        def store(n, values):
            at = PAIR_ROWS + n * TROWS
            stage[:, at : at + TROWS] = values.reshape(GROUPS, TROWS, HD).astype(BF16)

        for h in range(NH):
            cut = slice(h * HD, (h + 1) * HD)
            if h < NF:
                key_grad = tacc_ref[0, :, cut] + text0_ref[0, :, cut]
                value_grad = tacc_ref[1, :, cut] + text0_ref[1, :, cut]
            else:
                key_grad, value_grad = tk_acc[...], tv_acc[...]
            store(h, tqg_ref[:, cut])
            store(NH + h, key_grad * FACTOR)
            store(2 * NH + h, value_grad)
    for g in range(GROUPS):
        for m in range(MOST):
            slot = TILES + g * MOST + m
            stage[g, 2 * m * TILE : (2 * m + 1) * TILE] = (dk_acc[slot] * FACTOR).astype(BF16)
            stage[g, (2 * m + 1) * TILE : (2 * m + 2) * TILE] = dv_acc[slot].astype(BF16)
        stores += go([pltpu.make_async_copy(stage.at[g], back_ref.at[g], back_sems.at[g])])
    finish(stores)


def video(first, slot, count, n, x, got, tk, tv, *text):
    heads = NF if first else NH - NF
    rows = PAIR_ROWS if first else BACK_REST
    width = heads * HD
    pair = (TILES, 2, TILE, width)
    in_specs = [pl.BlockSpec(memory_space=SMEM)] * 3 + any_specs(2) + [whole(TEXT)] * 2
    out_specs = [whole(pair)] + any_specs(2)
    out_shape = [
        jax.ShapeDtypeStruct(pair, BF16),
        jax.ShapeDtypeStruct((GROUPS, rows, width), BF16),
        jax.ShapeDtypeStruct(pair, F32),
    ]
    if first:
        out_specs.append(whole((2, TXT, WF)))
        out_shape.append(jax.ShapeDtypeStruct((2, TXT, WF), F32))
    else:
        in_specs += [whole(TEXT), whole((2, TXT, W)), whole((2, TXT, WF))]
    return pl.pallas_call(
        functools.partial(video_kernel, first),
        grid=(1,),
        in_specs=in_specs,
        out_specs=out_specs,
        out_shape=out_shape,
        scratch_shapes=[
            pltpu.VMEM((CHUNKS, 256, width), BF16),
            pltpu.VMEM((CHUNKS, 256, width), BF16),
            pltpu.VMEM((heads, CHUNKS, 256, TILE), F32),
            pltpu.VMEM((heads, CHUNKS, 256, TILE), BF16),
            pltpu.VMEM((POOL, TILE, width), F32),
            pltpu.VMEM((POOL, TILE, width), F32),
            pltpu.VMEM((TXT, width), F32),
            pltpu.VMEM((TXT, width), F32),
            pltpu.VMEM((POOL * 2 * TILE, width), BF16),
            pltpu.VMEM(pair, BF16),
            pltpu.VMEM((GROUPS, rows, width), BF16),
            pltpu.SemaphoreType.DMA((TILES, 2)),
            pltpu.SemaphoreType.DMA((GROUPS,)),
            pltpu.SemaphoreType.DMA,
            pltpu.SemaphoreType.DMA((GROUPS,)),
            pltpu.SemaphoreType.DMA((2,)),
        ],
        compiler_params=params(),
        cost_estimate=cost(
            12 * heads * TLOCAL * 1280 * HD, heads * (8 << 20), heads * TLOCAL * 1280
        ),
        name="video_first" if first else "video_rest",
    )(slot, count, n, x, got, tk, tv, *text)


def combine_kernel(sel_ref, back_ref, own_ref, dx_ref, half_ref, *refs):
    out_ref, acc = refs[-2:]
    acc[:, 0] = (own_ref[:, 0] + dx_ref[:, 0]) * FACTOR
    acc[:, 1] = own_ref[:, 1] + dx_ref[:, 1]

    def add(g, carry):
        for m in range(MOST):
            at = sel_ref[g * MOST + m]
            part = back_ref[g, 2 * m * TILE : 2 * (m + 1) * TILE].astype(F32)
            acc[at] += part.reshape(2, TILE, HD)
        return carry

    lax.fori_loop(0, GROUPS, add, 0)
    out_ref[:, :2] = half_ref[...]
    out_ref[:, 2:] = acc[...].astype(BF16)


def combine(first, sel, back, own, dx, half, *packed):
    base, heads = (0, NF) if first else (NF, NH - NF)
    pair = (TILES, 2, TILE, HD)
    return pl.pallas_call(
        combine_kernel,
        grid=(heads,),
        in_specs=[
            pl.BlockSpec(memory_space=SMEM),
            pl.BlockSpec((GROUPS, PAIR_ROWS, HD), lambda j: (0, 0, j)),
            pl.BlockSpec(pair, lambda j: (0, 0, 0, j)),
            pl.BlockSpec(pair, lambda j: (0, 0, 0, base + j)),
            pl.BlockSpec(pair, lambda j: (0, 0, 0, j)),
        ]
        + any_specs(len(packed)),
        out_specs=pl.BlockSpec((TILES, 4, TILE, HD), lambda j: (0, 0, 0, base + j)),
        out_shape=jax.ShapeDtypeStruct((TILES, 4, TILE, W), BF16),
        scratch_shapes=[pltpu.VMEM(pair, F32)],
        input_output_aliases={5: 0} if packed else {},
        compiler_params=params(),
        cost_estimate=cost(heads * TLOCAL * HD * 64, heads * (5 << 20)),
        name="combine_first" if first else "combine_rest",
    )(sel, back, own, dx, half, *packed)


def text_sum_kernel(back_ref, out_ref, o_ref, rows, sem):
    load = [pltpu.make_async_copy(back_ref.at[:, pl.ds(PAIR_ROWS, 3 * NH * TROWS)], rows, sem)]
    finish(go(load))
    total = jnp.sum(rows[...].astype(F32), axis=0).astype(BF16)
    o_ref[0] = out_ref[...]
    for n in range(3 * NH):
        h = n % NH
        o_ref[n // NH + 1, :, h * HD : (h + 1) * HD] = total[n * TROWS : (n + 1) * TROWS]


def text_sum(back, out):
    return pl.pallas_call(
        text_sum_kernel,
        grid=(1,),
        in_specs=any_specs(1) + [whole((TROWS, W))],
        out_specs=whole((4, TROWS, W)),
        out_shape=jax.ShapeDtypeStruct((4, TROWS, W), BF16),
        scratch_shapes=[
            pltpu.VMEM((GROUPS, 3 * NH * TROWS, WR), BF16),
            pltpu.SemaphoreType.DMA,
        ],
        compiler_params=params(),
        cost_estimate=cost(GROUPS * 9 * TROWS * WR, 1 << 20),
        name="text_sum",
    )(back, out)


STEPS = ((1, 1), (2, 2), (4, 6), (8, 8))


def swapped(x, mask):
    return lax.ppermute(x, "seq", [(i, i ^ mask) for i in range(GROUPS)])


def tables(tile_list, tile_count, own):
    live = jnp.arange(KT)[None, :] < tile_count[:, None]
    listed = jnp.where(live, tile_list, -1)

    def ranked(wanted):
        before = jnp.arange(TILES)[:, None] < jnp.arange(TILES)[None, :]
        return jnp.sum(jnp.where(before[None], wanted[:, :, None], 0), axis=1)

    mine = own * TILES + jnp.arange(TILES)
    asked = jnp.any(
        listed.reshape(GROUPS, TILES * KT, 1) == mine[None, None, :], axis=1
    ).astype(jnp.int32)
    rank = ranked(asked)
    chosen = (asked[:, None, :] > 0) & (rank[:, None, :] == jnp.arange(MOST)[None, :, None])
    sel = jnp.sum(jnp.where(chosen, jnp.arange(TILES)[None, None, :], 0), axis=2).reshape(SLOTS)

    my_list = lax.dynamic_slice_in_dim(listed, own * TILES, TILES, 0).reshape(TILES * KT)
    hits = my_list[:, None] == jnp.arange(GROUPS * TILES)[None, :]
    needed = jnp.any(hits, axis=0).astype(jnp.int32).reshape(GROUPS, TILES)
    where_to = TILES + jnp.arange(GROUPS)[:, None] * MOST + jnp.minimum(ranked(needed), MOST - 1)
    local = jnp.arange(GROUPS)[:, None] == own
    where_to = jnp.where(local, jnp.arange(TILES)[None, :], where_to).reshape(GROUPS * TILES)
    slot = jnp.sum(jnp.where(hits, where_to[None, :], 0), axis=1)
    count = lax.dynamic_slice_in_dim(tile_count, own * TILES, TILES, 0)
    return sel.astype(jnp.int32), slot.astype(jnp.int32), count.astype(jnp.int32)


def body(
    video_query,
    video_key,
    video_value,
    video_grad,
    text_query,
    text_key,
    text_value,
    text_grad,
    tile_list,
    tile_count,
    text_mask,
):
    own = lax.axis_index("seq")
    x = lax.all_to_all(
        pack(video_key, video_value, video_query, video_grad), "head", 0, 0, tiled=True
    )
    sel, slot, count = tables(tile_list, tile_count, own)
    n = jnp.sum((text_mask > 0).astype(jnp.int32)).reshape(1)
    n_own = jnp.where(own == 0, n, 0)
    sel, slot, count, n, n_own = lax.optimization_barrier((sel, slot, count, n, n_own))
    text = (text_query, text_key, text_value)

    send0, send1 = send(sel, n_own, *text, x)
    got0 = lax.all_to_all(send0, "seq", 0, 0, tiled=True)
    send1, text_out = text_stats(own.reshape(1), got0, text_grad, send1)
    got = lax.all_to_all(send1, "seq", 0, 0, tiled=True)
    half0, back0, own0, text0 = video(
        True, slot, count, n, x, got0, text_key, text_value
    )
    back0 = lax.all_to_all(back0, "seq", 0, 0, tiled=True)
    tqg, tacc, dx = text_backward(n_own, got, *text, text_grad, x)
    half, back, own_grads = video(
        False, slot, count, n, x, got, text_key, text_value, tqg, tacc, text0
    )
    back = lax.all_to_all(back, "seq", 0, 0, tiled=True)
    packed = combine(True, sel, back0, own0, dx, half0)
    packed = combine(False, sel, back, own_grads, dx, half, packed)

    gathered = text_sum(back, text_out)[None]
    for bit, mask in STEPS:
        theirs = swapped(gathered, mask)
        first = jnp.concatenate([gathered, theirs], axis=0)
        second = jnp.concatenate([theirs, gathered], axis=0)
        gathered = jnp.where((own & bit) == 0, first, second)
    text_rows = jnp.transpose(gathered, (1, 0, 2, 3)).reshape(4, TXT, W)

    attended_video, video_query_grad, video_key_grad, video_value_grad = unpack(
        lax.all_to_all(packed, "head", 0, 0, tiled=True)
    )
    return (
        attended_video,
        video_query_grad,
        video_key_grad,
        video_value_grad,
        text_rows[0],
        text_rows[1],
        text_rows[2],
        text_rows[3],
    )


def solution(mesh):
    tokens, heads = P(("seq", "head"), None), P(None, "head")
    return jax.shard_map(
        body,
        mesh=mesh,
        in_specs=(tokens,) * 4 + (heads,) * 4 + (P(),) * 3,
        out_specs=(tokens,) * 4 + (heads,) * 4,
        check_vma=False,
    )
```

```python
import functools

import jax
import jax.numpy as jnp
from jax import lax
from jax.experimental import pallas as pl
from jax.experimental.pallas import tpu as pltpu
from jax.sharding import PartitionSpec as P

HD = 128
TXT = 256
TILE = 128
KT = 8
MOST = 2
GROUPS = 16
HEADS = 8
TILES = 8
NH = 3
W = NH * HD
SLOTS = GROUPS * MOST
POOL = TILES + SLOTS
TROWS = TXT // GROUPS
TLOCAL = TILES * TILE
TCHUNKS = TLOCAL // 256 + 1
PAIR_ROWS = MOST * 2 * TILE
SEND_FIRST = PAIR_ROWS + 2 * TROWS
SEND_REST = PAIR_ROWS + TROWS
BACK_REST = PAIR_ROWS + 5 * TROWS
NF = 2
WF = NF * HD
WR = W - WF

NEGATIVE = -1e30
FACTOR = HD**-0.5
LOG2E = 1.4426950408889634
FACTOR2 = FACTOR * LOG2E
VMEM_LIMIT = 67043328

F32 = jnp.float32
BF16 = jnp.bfloat16
SMEM = pltpu.SMEM
ANY = pl.ANY


def dot_nt(a, b):
    return lax.dot_general(a, b, (((1,), (1,)), ((), ())), preferred_element_type=F32)


def dot_nn(a, b):
    return lax.dot_general(a, b, (((1,), (0,)), ((), ())), preferred_element_type=F32)


def dot_tn(a, b):
    return lax.dot_general(a, b, (((0,), (0,)), ((), ())), preferred_element_type=F32)


def params(**kw):
    return pltpu.CompilerParams(vmem_limit_bytes=VMEM_LIMIT, **kw)


def cost(flops, nbytes, exps=0):
    return pl.CostEstimate(
        flops=int(flops), bytes_accessed=int(nbytes), transcendentals=int(exps)
    )


def go(copies):
    for copy in copies:
        copy.start()
    return copies


def finish(copies):
    for copy in copies:
        copy.wait()


def columns(h):
    return pl.ds(h * W, W)


def pack_kernel(k_ref, v_ref, q_ref, g_ref, o_ref, rows, in_sems, out_sems):
    refs = (k_ref, v_ref, q_ref, g_ref)
    loads = go([pltpu.make_async_copy(refs[n], rows.at[n], in_sems.at[n]) for n in range(4)])
    stores = []
    for n in range(4):
        loads[n].wait()
        stores += go(
            [
                pltpu.make_async_copy(
                    rows.at[n, :, columns(h)], o_ref.at[h, n], out_sems.at[n, h]
                )
                for h in range(HEADS)
            ]
        )
    finish(stores)


def any_specs(n):
    return [pl.BlockSpec(memory_space=ANY)] * n


def pack(k, v, q, g):
    return pl.pallas_call(
        pack_kernel,
        in_specs=any_specs(4),
        out_specs=pl.BlockSpec(memory_space=ANY),
        out_shape=jax.ShapeDtypeStruct((HEADS, 4, TILE, W), BF16),
        scratch_shapes=[
            pltpu.VMEM((4, TILE, HEADS * W), BF16),
            pltpu.SemaphoreType.DMA((4,)),
            pltpu.SemaphoreType.DMA((4, HEADS)),
        ],
        compiler_params=params(),
        cost_estimate=cost(0, 8 * TILE * HEADS * W * 2),
        name="pack",
    )(k, v, q, g)


def unpack_kernel(x_ref, a_ref, b_ref, c_ref, d_ref, rows, in_sems, out_sems):
    refs = (a_ref, b_ref, c_ref, d_ref)
    loads = [
        go(
            [
                pltpu.make_async_copy(
                    x_ref.at[h, n], rows.at[n, :, columns(h)], in_sems.at[n, h]
                )
                for h in range(HEADS)
            ]
        )
        for n in range(4)
    ]
    stores = []
    for n in range(4):
        finish(loads[n])
        stores += go([pltpu.make_async_copy(rows.at[n], refs[n], out_sems.at[n])])
    finish(stores)


def unpack(x):
    return pl.pallas_call(
        unpack_kernel,
        in_specs=any_specs(1),
        out_specs=any_specs(4),
        out_shape=[jax.ShapeDtypeStruct((TILE, HEADS * W), BF16)] * 4,
        scratch_shapes=[
            pltpu.VMEM((4, TILE, HEADS * W), BF16),
            pltpu.SemaphoreType.DMA((4, HEADS)),
            pltpu.SemaphoreType.DMA((4,)),
        ],
        compiler_params=params(),
        cost_estimate=cost(0, 8 * TILE * HEADS * W * 2),
        name="unpack",
    )(x)


def picked(sel_ref, x_ref, o_ref, sems, lanes):
    return [
        pltpu.make_async_copy(
            x_ref.at[sel_ref[g * MOST + m], kv, :, lanes],
            o_ref.at[g, pl.ds((2 * m + kv) * TILE, TILE)],
            sems.at[g, 2 * m + kv],
        )
        for g in range(GROUPS)
        for m in range(MOST)
        for kv in range(2)
    ]


def text_chunk(x_ref, text_ref, which, c, lanes):
    if c < TCHUNKS - 1:
        return x_ref[2 * c : 2 * c + 2, which, :, lanes].reshape(256, HD)
    return text_ref[:, lanes]


def head_lanes(j):
    return pl.ds(pl.multiple_of(j * HD, HD), HD)


def whole(shape):
    return pl.BlockSpec(shape, lambda i: (0,) * len(shape))


TEXT = (TXT, W)
LOCAL_KV = (TILES, 2, TILE, W)


def thirds(x):
    first = x.astype(BF16).astype(F32)
    second = (x - first).astype(BF16).astype(F32)
    return first, second, x - first - second


def put(lane, block, at, column):
    return jnp.where(lane == at, column, block)


def take(lane, block, low, high, j):
    hit = (lane >= low) & (lane < high) & (lane % 8 == j)
    return jnp.sum(jnp.where(hit, block, 0.0), axis=1, keepdims=True)


def send_kernel(
    sel_ref,
    n_ref,
    tq_ref,
    tk_ref,
    tv_ref,
    x_ref,
    o_ref,
    rest_ref,
    s_ref,
    part_ref,
    sems,
    rest_sems,
    part_sem,
):
    def put_part(n, rows):
        at, lanes = n // 2 * TROWS, slice(n % 2 * HD, (n % 2 + 1) * HD)
        part_ref[:, at : at + TROWS, lanes] = rows.astype(BF16).reshape(GROUPS, TROWS, HD)

    tiles = go(picked(sel_ref, x_ref, o_ref, sems, pl.ds(0, WF)))
    tiles += go(picked(sel_ref, x_ref, rest_ref, rest_sems, pl.ds(WF, WR)))
    live = lax.broadcasted_iota(jnp.int32, (TXT, TXT), 1) < n_ref[0]
    lane = lax.broadcasted_iota(jnp.int32, (TXT, HD), 1)
    stats = jnp.zeros((TXT, HD), F32)
    for j in range(NH):
        lanes = slice(j * HD, (j + 1) * HD)
        query = tq_ref[:, lanes]
        top = None
        for c in range(TCHUNKS):
            s = dot_nt(query, text_chunk(x_ref, tk_ref, 0, c, lanes)) * FACTOR2
            if c == TCHUNKS - 1:
                s = jnp.where(live, s, NEGATIVE)
            s_ref[c] = s
            top = s if top is None else jnp.maximum(top, s)
        top = jnp.max(top, axis=1, keepdims=True).astype(BF16).astype(F32)
        total, out = None, None
        for c in range(TCHUNKS):
            p = jnp.exp2(s_ref[c] - top)
            part = dot_nn(p.astype(BF16), text_chunk(x_ref, tv_ref, 1, c, lanes))
            total = p if total is None else total + p
            out = part if out is None else out + part
        total = jnp.sum(total, axis=1, keepdims=True)
        put_part(j, out)
        stats = put(lane, stats, j, top)
        for n, third in enumerate(thirds(total)):
            stats = put(lane, stats, 8 * (n + 1) + j, third)
    put_part(NH, stats)
    parts = go(
        [pltpu.make_async_copy(part_ref, o_ref.at[:, pl.ds(PAIR_ROWS, 2 * TROWS)], part_sem)]
    )
    finish(tiles + parts)


def send(sel, n, tq, tk, tv, x):
    return pl.pallas_call(
        send_kernel,
        grid=(1,),
        in_specs=[pl.BlockSpec(memory_space=SMEM)] * 2 + [whole(TEXT)] * 3 + [whole(LOCAL_KV)],
        out_specs=any_specs(2),
        out_shape=[
            jax.ShapeDtypeStruct((GROUPS, SEND_FIRST, WF), BF16),
            jax.ShapeDtypeStruct((GROUPS, SEND_REST, WR), BF16),
        ],
        scratch_shapes=[
            pltpu.VMEM((TCHUNKS, TXT, 256), F32),
            pltpu.VMEM((GROUPS, 2 * TROWS, WF), BF16),
            pltpu.SemaphoreType.DMA((GROUPS, 2 * MOST)),
            pltpu.SemaphoreType.DMA((GROUPS, 2 * MOST)),
            pltpu.SemaphoreType.DMA,
        ],
        compiler_params=params(),
        cost_estimate=cost(4 * NH * TXT * TCHUNKS * 256 * HD, 5 << 20, NH * TXT * 1280),
        name="send",
    )(sel, n, tq, tk, tv, x)


def text_stats_kernel(own_ref, got_ref, tg_ref, in_ref, o_ref, out_ref, parts, tg, stats_ref, sems):
    mine = pl.ds(pl.multiple_of(own_ref[0] * TROWS, TROWS), TROWS)
    load = go(
        [
            pltpu.make_async_copy(
                got_ref.at[:, pl.ds(PAIR_ROWS, 2 * TROWS)], parts, sems.at[0]
            ),
            pltpu.make_async_copy(tg_ref.at[mine], tg, sems.at[1]),
        ]
    )
    lane_all = lax.broadcasted_iota(jnp.int32, (TXT, HD), 1)
    lane = lax.broadcasted_iota(jnp.int32, (TROWS, HD), 1)
    finish(load)
    received = parts[:, TROWS:, HD:].astype(F32).reshape(TXT, HD)
    stats = jnp.zeros((TROWS, HD), F32)
    for j in range(NH):
        lanes = slice(j * HD, (j + 1) * HD)
        tops = take(lane_all, received, 0, 8, j).reshape(GROUPS, TROWS, 1)
        totals = take(lane_all, received, 8, 32, j).reshape(GROUPS, TROWS, 1)
        top = jnp.max(tops, axis=0)
        scale = jnp.exp2(tops - top[None])
        total = jnp.sum(scale * totals, axis=0)
        part = parts[:, j // 2 * TROWS : (j // 2 + 1) * TROWS, j % 2 * HD : (j % 2 + 1) * HD]
        out = jnp.sum(scale * part.astype(F32), axis=0) / total
        out_ref[:, lanes] = out.astype(BF16)
        offset = jnp.sum(tg[:, lanes].astype(F32) * out, axis=1, keepdims=True)
        for n, third in enumerate(thirds(top + jnp.log2(total)) + thirds(offset)):
            stats = put(lane, stats, 8 * n + j, third)
    stats_ref[...] = jnp.broadcast_to(stats.astype(BF16)[None], (GROUPS, TROWS, HD))
    finish(
        go([pltpu.make_async_copy(stats_ref, o_ref.at[:, pl.ds(PAIR_ROWS, TROWS)], sems.at[2])])
    )


def text_stats(own, got, tg, send):
    return pl.pallas_call(
        text_stats_kernel,
        grid=(1,),
        in_specs=[pl.BlockSpec(memory_space=SMEM)] + any_specs(3),
        out_specs=[pl.BlockSpec(memory_space=ANY), whole((TROWS, W))],
        out_shape=[
            jax.ShapeDtypeStruct(send.shape, BF16),
            jax.ShapeDtypeStruct((TROWS, W), BF16),
        ],
        scratch_shapes=[
            pltpu.VMEM((GROUPS, 2 * TROWS, WF), BF16),
            pltpu.VMEM((TROWS, W), BF16),
            pltpu.VMEM((GROUPS, TROWS, WR), BF16),
            pltpu.SemaphoreType.DMA((3,)),
        ],
        input_output_aliases={3: 0},
        compiler_params=params(),
        cost_estimate=cost(TXT * W * 8, 1 << 19),
        name="text_stats",
    )(own, got, tg, send)


def text_backward_kernel(
    n_ref, got_ref, tq_ref, tk_ref, tv_ref, tg_ref, x_ref, own_ref, tqg_ref, acc_ref, dx_ref, rows, sem
):
    load = go(
        [
            pltpu.make_async_copy(
                got_ref.at[:, pl.ds(PAIR_ROWS, TROWS), pl.ds(0, HD)], rows, sem
            )
        ]
    )
    live = lax.broadcasted_iota(jnp.int32, (TXT, TXT), 1) < n_ref[0]
    lane = lax.broadcasted_iota(jnp.int32, (TXT, HD), 1)
    finish(load)

    def head(j, carry):
        lanes = head_lanes(j)
        stats = rows[...].astype(F32).reshape(TXT, HD)
        log_total = take(lane, stats, 0, 24, j)
        offset = take(lane, stats, 24, 48, j)
        query, grad = tq_ref[:, lanes], tg_ref[:, lanes]
        query_grad = None
        for c in range(TCHUNKS):
            key = text_chunk(x_ref, tk_ref, 0, c, lanes)
            value = text_chunk(x_ref, tv_ref, 1, c, lanes)
            s = dot_nt(query, key) * FACTOR2
            if c == TCHUNKS - 1:
                s = jnp.where(live, s, NEGATIVE)
            p = jnp.exp2(s - log_total)
            ds = (p * (dot_nt(grad, value) - offset)).astype(BF16)
            p = p.astype(BF16)
            part = dot_nn(ds, key)
            query_grad = part if query_grad is None else query_grad + part
            key_grad = dot_tn(ds, query)
            value_grad = dot_tn(p, grad)
            if c < TCHUNKS - 1:
                dx_ref[2 * c : 2 * c + 2, 0, :, lanes] = key_grad.reshape(2, TILE, HD)
                dx_ref[2 * c : 2 * c + 2, 1, :, lanes] = value_grad.reshape(2, TILE, HD)
            else:
                acc_ref[0, :, lanes] = key_grad
                acc_ref[1, :, lanes] = value_grad
        tqg_ref[:, lanes] = query_grad * FACTOR
        return carry

    lax.fori_loop(0, NH, head, 0)
    for t in range(TILES):
        dx_ref[t, :, :, :WF] += own_ref[t]


def text_backward(n, got, tq, tk, tv, tg, x, own):
    return pl.pallas_call(
        text_backward_kernel,
        grid=(1,),
        in_specs=[pl.BlockSpec(memory_space=SMEM)]
        + any_specs(1)
        + [whole(TEXT)] * 4
        + [whole(LOCAL_KV), whole((TILES, 2, TILE, WF))],
        out_specs=[whole(TEXT), whole((2, TXT, W)), whole(LOCAL_KV)],
        out_shape=[
            jax.ShapeDtypeStruct(TEXT, F32),
            jax.ShapeDtypeStruct((2, TXT, W), F32),
            jax.ShapeDtypeStruct(LOCAL_KV, F32),
        ],
        scratch_shapes=[
            pltpu.VMEM((GROUPS, TROWS, HD), BF16),
            pltpu.SemaphoreType.DMA,
        ],
        compiler_params=params(),
        cost_estimate=cost(10 * NH * TXT * TCHUNKS * 256 * HD, 8 << 20, NH * TXT * 1280),
        name="text_backward",
    )(n, got, tq, tk, tv, tg, x, own)


CHUNKS = KT // 2 + 1


def video_kernel(
    first, slot_ref, count_ref, n_ref, x_ref, got_ref, tk_ref, tv_ref, *refs
):
    if first:
        packed_ref, back_ref, own_ref, both_ref, text_ref = refs[:5]
        refs = refs[5:]
    else:
        tqg_ref, tacc_ref, text0_ref, dx_ref = refs[:4]
        packed_ref, both_ref, own_ref = refs[6:9]
        refs = refs[9:]
    keys, values, s_ref, p_ref, dk_acc, dv_acc, tk_acc, tv_acc, pool, qg, out_ref, stage = refs[:12]
    text_stage, kv_sems, got_sems, qg_sem, back_sems, own_sems, dx_sems, out_sems = refs[12:]
    base, heads = (0, NF) if first else (NF, NH - NF)
    mine = slice(base * HD, (base + heads) * HD)
    lanes = pl.ds(base * HD, heads * HD)

    def pool_rows(slot, kv):
        return pl.ds(pl.multiple_of((2 * slot + kv) * TILE, TILE), TILE)

    loads = [
        pltpu.make_async_copy(
            x_ref.at[t, kv, :, lanes], pool.at[pool_rows(t, kv)], kv_sems.at[t, kv]
        )
        for t in range(TILES)
        for kv in range(2)
    ]
    loads.append(pltpu.make_async_copy(x_ref.at[:, pl.ds(2, 2), :, lanes], qg, qg_sem))
    loads += [
        pltpu.make_async_copy(
            got_ref.at[g, pl.ds(0, PAIR_ROWS)],
            pool.at[pl.ds(2 * TILES * TILE + g * PAIR_ROWS, PAIR_ROWS)],
            got_sems.at[g],
        )
        for g in range(GROUPS)
    ]
    if not first:
        loads += [
            pltpu.make_async_copy(
                dx_ref.at[:, n, :, lanes], acc.at[pl.ds(0, TILES)], dx_sems.at[n]
            )
            for n, acc in enumerate((dk_acc, dv_acc))
        ]
    go(loads)
    keys[0] = tk_ref[:, mine]
    values[0] = tv_ref[:, mine]

    def clear(slot, carry):
        dk_acc[slot] = jnp.zeros((TILE, heads * HD), F32)
        dv_acc[slot] = jnp.zeros((TILE, heads * HD), F32)
        return carry

    lax.fori_loop(0 if first else TILES, POOL, clear, 0)
    if first:
        tk_acc[...] = jnp.zeros((TXT, heads * HD), F32)
        tv_acc[...] = jnp.zeros((TXT, heads * HD), F32)
    else:
        tk_acc[...] = tacc_ref[0, :, mine]
        tv_acc[...] = tacc_ref[1, :, mine]
    text_live = lax.broadcasted_iota(jnp.int32, (TXT, TILE), 0) < n_ref[0]
    finish(loads)
    cuts = [slice(h * HD, (h + 1) * HD) for h in range(heads)]

    def tile(i, carry):
        count = count_ref[i]

        def run(pairs):
            slots = [slot_ref[i * KT + e] for e in range(2 * pairs)]
            for e in range(2 * pairs):
                half = pl.ds((e % 2) * TILE, TILE)
                keys[1 + e // 2, half] = pool[pool_rows(slots[e], 0)]
                values[1 + e // 2, half] = pool[pool_rows(slots[e], 1)]
            query = [qg[i, 0, :, cut] for cut in cuts]
            grad = [qg[i, 1, :, cut] for cut in cuts]
            tops, scales, offsets = [], [], []
            for h, cut in enumerate(cuts):
                top = None
                for c in range(pairs + 1):
                    s = dot_nt(keys[c, :, cut], query[h]) * FACTOR2
                    if c == 0:
                        s = jnp.where(text_live, s, NEGATIVE)
                    elif c == pairs:
                        dead = jnp.where(2 * pairs <= count, s[TILE:], NEGATIVE)
                        s = jnp.concatenate([s[:TILE], dead], axis=0)
                    s_ref[h, c] = s
                    part = jnp.max(s.reshape(32, 8, TILE), axis=0)
                    top = part if top is None else jnp.maximum(top, part)
                tops.append(jnp.max(top, axis=0, keepdims=True))
            for h, cut in enumerate(cuts):
                total = None
                for c in range(pairs + 1):
                    p = jnp.exp2(s_ref[h, c] - tops[h])
                    s_ref[h, c] = p
                    part = jnp.sum(p.reshape(32, 8, TILE), axis=0)
                    total = part if total is None else total + part
                scales.append(1.0 / jnp.sum(total, axis=0, keepdims=True))
            for h, cut in enumerate(cuts):
                out = None
                for c in range(pairs + 1):
                    p = s_ref[h, c] * scales[h]
                    s_ref[h, c] = p
                    p = p.astype(BF16)
                    p_ref[h, c] = p
                    part = dot_tn(p, values[c, :, cut])
                    out = part if out is None else out + part
                out_ref[i, 0, :, cut] = out.astype(BF16)
                offsets.append(
                    jnp.sum((grad[h].astype(F32) * out).T, axis=0, keepdims=True)
                )
            for h, cut in enumerate(cuts):
                query_grad = None
                for c in range(pairs + 1):
                    dp = dot_nt(values[c, :, cut], grad[h])
                    ds = (s_ref[h, c] * (dp - offsets[h])).astype(BF16)
                    part = dot_tn(ds, keys[c, :, cut])
                    query_grad = part if query_grad is None else query_grad + part
                    key_grad = dot_nn(ds, query[h])
                    value_grad = dot_nn(p_ref[h, c], grad[h])
                    if c == 0:
                        tk_acc[:, cut] += key_grad
                        tv_acc[:, cut] += value_grad
                    else:
                        for e in (0, 1):
                            slot = slots[2 * (c - 1) + e]
                            rows = slice(e * TILE, (e + 1) * TILE)
                            dk_acc[slot, :, cut] += key_grad[rows]
                            dv_acc[slot, :, cut] += value_grad[rows]
                out_ref[i, 1, :, cut] = (query_grad * FACTOR).astype(BF16)

        for pairs in range(1, KT // 2 + 1):

            @pl.when((count + 1) // 2 == pairs)
            def _():
                run(pairs)

        return carry

    lax.fori_loop(0, TILES, tile, 0)

    stores = go(
        [
            pltpu.make_async_copy(acc.at[pl.ds(0, TILES)], own_ref.at[:, n], own_sems.at[n])
            for n, acc in enumerate((dk_acc, dv_acc))
        ]
        + [
            pltpu.make_async_copy(
                out_ref, packed_ref.at[:, pl.ds(0, 2), :, lanes], out_sems.at[0]
            )
        ]
    )
    if first:
        text_ref[0] = tk_acc[...]
        text_ref[1] = tv_acc[...]
    else:

        def store(n, values):
            at, cut = n // 2 * TROWS, slice(n % 2 * HD, (n % 2 + 1) * HD)
            values = values.reshape(GROUPS, TROWS, HD).astype(BF16)
            text_stage[:, at : at + TROWS, cut] = values

        for h in range(NH):
            cut = slice(h * HD, (h + 1) * HD)
            if h < NF:
                key_grad = tacc_ref[0, :, cut] + text0_ref[0, :, cut]
                value_grad = tacc_ref[1, :, cut] + text0_ref[1, :, cut]
            else:
                key_grad, value_grad = tk_acc[...], tv_acc[...]
            store(h, tqg_ref[:, cut])
            store(NH + h, key_grad * FACTOR)
            store(2 * NH + h, value_grad)
        store(3 * NH, jnp.zeros((TXT, HD), F32))
        stores += go(
            [
                pltpu.make_async_copy(
                    text_stage, both_ref.at[:, pl.ds(PAIR_ROWS, 5 * TROWS)], out_sems.at[1]
                )
            ]
        )
    pair_rows = pl.ds(0, PAIR_ROWS)
    for g in range(GROUPS):
        for m in range(MOST):
            slot = TILES + g * MOST + m
            stage[g, 2 * m * TILE : (2 * m + 1) * TILE] = (dk_acc[slot] * FACTOR).astype(BF16)
            stage[g, (2 * m + 1) * TILE : (2 * m + 2) * TILE] = dv_acc[slot].astype(BF16)
        if first:
            targets = (back_ref.at[g], both_ref.at[g, pair_rows, pl.ds(0, HD)])
        else:
            targets = (both_ref.at[g, pair_rows, pl.ds(HD, HD)],)
        stores += go(
            [
                pltpu.make_async_copy(
                    stage.at[g, :, pl.ds(n * HD, HD)], target, back_sems.at[g, n]
                )
                for n, target in enumerate(targets)
            ]
        )
    finish(stores)


def video(first, slot, count, n, x, got, tk, tv, *text):
    heads = NF if first else NH - NF
    width = heads * HD
    pair = (TILES, 2, TILE, width)
    in_specs = [pl.BlockSpec(memory_space=SMEM)] * 3 + any_specs(2) + [whole(TEXT)] * 2
    packed = jax.ShapeDtypeStruct((TILES, 4, TILE, W), BF16)
    both = jax.ShapeDtypeStruct((GROUPS, BACK_REST, 2 * HD), BF16)
    own = jax.ShapeDtypeStruct(pair, F32)
    if first:
        out_specs = any_specs(4) + [whole((2, TXT, WF))]
        back = jax.ShapeDtypeStruct((GROUPS, PAIR_ROWS, HD), BF16)
        out_shape = [packed, back, own, both, jax.ShapeDtypeStruct((2, TXT, WF), F32)]
        aliases = {}
    else:
        in_specs += [whole(TEXT), whole((2, TXT, W)), whole((2, TXT, WF))] + any_specs(3)
        out_specs = any_specs(3)
        out_shape = [packed, both, own]
        aliases = {11: 0, 12: 1}
    return pl.pallas_call(
        functools.partial(video_kernel, first),
        grid=(1,),
        in_specs=in_specs,
        out_specs=out_specs,
        out_shape=out_shape,
        scratch_shapes=[
            pltpu.VMEM((CHUNKS, 256, width), BF16),
            pltpu.VMEM((CHUNKS, 256, width), BF16),
            pltpu.VMEM((heads, CHUNKS, 256, TILE), F32),
            pltpu.VMEM((heads, CHUNKS, 256, TILE), BF16),
            pltpu.VMEM((POOL, TILE, width), F32),
            pltpu.VMEM((POOL, TILE, width), F32),
            pltpu.VMEM((TXT, width), F32),
            pltpu.VMEM((TXT, width), F32),
            pltpu.VMEM((POOL * 2 * TILE, width), BF16),
            pltpu.VMEM(pair, BF16),
            pltpu.VMEM(pair, BF16),
            pltpu.VMEM((GROUPS, PAIR_ROWS, width), BF16),
            pltpu.VMEM((GROUPS, 5 * TROWS, 2 * HD), BF16),
            pltpu.SemaphoreType.DMA((TILES, 2)),
            pltpu.SemaphoreType.DMA((GROUPS,)),
            pltpu.SemaphoreType.DMA,
            pltpu.SemaphoreType.DMA((GROUPS, 2)),
            pltpu.SemaphoreType.DMA((2,)),
            pltpu.SemaphoreType.DMA((2,)),
            pltpu.SemaphoreType.DMA((2,)),
        ],
        input_output_aliases=aliases,
        compiler_params=params(),
        cost_estimate=cost(
            12 * heads * TLOCAL * 1280 * HD, heads * (8 << 20), heads * TLOCAL * 1280
        ),
        name="video_first" if first else "video_rest",
    )(slot, count, n, x, got, tk, tv, *text)


def combine_kernel(
    sel_ref, first_ref, both_ref, dx_ref, own_ref, in_ref, packed_ref, acc, back, out, own_sems, sems, out_sem
):
    loads = go(
        [
            pltpu.make_async_copy(
                dx_ref.at[:, :, :, pl.ds(0, WF)], acc.at[:, :, :, pl.ds(0, WF)], own_sems.at[0]
            ),
            pltpu.make_async_copy(own_ref, acc.at[:, :, :, pl.ds(WF, WR)], own_sems.at[1]),
        ]
    )

    def parts(g):
        rows = pl.ds(0, PAIR_ROWS)
        return [
            pltpu.make_async_copy(first_ref.at[g], back.at[g, :, pl.ds(0, HD)], sems.at[g, 0]),
            pltpu.make_async_copy(
                both_ref.at[g, rows], back.at[g, :, pl.ds(HD, 2 * HD)], sems.at[g, 1]
            ),
        ]

    for g in range(GROUPS):
        go(parts(g))
    finish(loads)
    for t in range(TILES):
        acc[t, 0] = acc[t, 0] * FACTOR

    def add(g, carry):
        finish(parts(g))
        for m in range(MOST):
            at = sel_ref[g * MOST + m]
            part = back[g, 2 * m * TILE : 2 * (m + 1) * TILE].astype(F32)
            acc[at] += part.reshape(2, TILE, W)
        return carry

    lax.fori_loop(0, GROUPS, add, 0)
    for t in range(TILES):
        out[t] = acc[t].astype(BF16)
    finish(go([pltpu.make_async_copy(out, packed_ref.at[:, pl.ds(2, 2)], out_sem)]))


def combine(sel, first, both, dx, own, packed):
    return pl.pallas_call(
        combine_kernel,
        grid=(1,),
        in_specs=[pl.BlockSpec(memory_space=SMEM)] + any_specs(5),
        out_specs=pl.BlockSpec(memory_space=ANY),
        out_shape=jax.ShapeDtypeStruct((TILES, 4, TILE, W), BF16),
        scratch_shapes=[
            pltpu.VMEM(LOCAL_KV, F32),
            pltpu.VMEM((GROUPS, PAIR_ROWS, W), BF16),
            pltpu.VMEM(LOCAL_KV, BF16),
            pltpu.SemaphoreType.DMA((2,)),
            pltpu.SemaphoreType.DMA((GROUPS, 2)),
            pltpu.SemaphoreType.DMA,
        ],
        input_output_aliases={5: 0},
        compiler_params=params(),
        cost_estimate=cost(TLOCAL * W * 64, 14 << 20),
        name="combine",
    )(sel, first, both, dx, own, packed)


def text_sum_kernel(back_ref, out_ref, o_ref, rows, sem):
    load = [pltpu.make_async_copy(back_ref.at[:, pl.ds(PAIR_ROWS, 5 * TROWS)], rows, sem)]
    finish(go(load))
    total = jnp.sum(rows[...].astype(F32), axis=0).astype(BF16)
    o_ref[0] = out_ref[...]
    for n in range(3 * NH):
        h = n % NH
        at, cut = n // 2 * TROWS, slice(n % 2 * HD, (n % 2 + 1) * HD)
        o_ref[n // NH + 1, :, h * HD : (h + 1) * HD] = total[at : at + TROWS, cut]


def text_sum(back, out):
    return pl.pallas_call(
        text_sum_kernel,
        grid=(1,),
        in_specs=any_specs(1) + [whole((TROWS, W))],
        out_specs=whole((4, TROWS, W)),
        out_shape=jax.ShapeDtypeStruct((4, TROWS, W), BF16),
        scratch_shapes=[
            pltpu.VMEM((GROUPS, 5 * TROWS, 2 * HD), BF16),
            pltpu.SemaphoreType.DMA,
        ],
        compiler_params=params(),
        cost_estimate=cost(GROUPS * 9 * TROWS * WR, 1 << 20),
        name="text_sum",
    )(back, out)


STEPS = ((1, 1), (2, 2), (4, 6), (8, 8))


def swapped(x, mask):
    return lax.ppermute(x, "seq", [(i, i ^ mask) for i in range(GROUPS)])


def tables(tile_list, tile_count, own):
    live = jnp.arange(KT)[None, :] < tile_count[:, None]
    listed = jnp.where(live, tile_list, -1)

    def ranked(wanted):
        before = jnp.arange(TILES)[:, None] < jnp.arange(TILES)[None, :]
        return jnp.sum(jnp.where(before[None], wanted[:, :, None], 0), axis=1)

    mine = own * TILES + jnp.arange(TILES)
    asked = jnp.any(
        listed.reshape(GROUPS, TILES * KT, 1) == mine[None, None, :], axis=1
    ).astype(jnp.int32)
    rank = ranked(asked)
    chosen = (asked[:, None, :] > 0) & (rank[:, None, :] == jnp.arange(MOST)[None, :, None])
    sel = jnp.sum(jnp.where(chosen, jnp.arange(TILES)[None, None, :], 0), axis=2).reshape(SLOTS)

    my_list = lax.dynamic_slice_in_dim(listed, own * TILES, TILES, 0).reshape(TILES * KT)
    hits = my_list[:, None] == jnp.arange(GROUPS * TILES)[None, :]
    needed = jnp.any(hits, axis=0).astype(jnp.int32).reshape(GROUPS, TILES)
    where_to = TILES + jnp.arange(GROUPS)[:, None] * MOST + jnp.minimum(ranked(needed), MOST - 1)
    local = jnp.arange(GROUPS)[:, None] == own
    where_to = jnp.where(local, jnp.arange(TILES)[None, :], where_to).reshape(GROUPS * TILES)
    slot = jnp.sum(jnp.where(hits, where_to[None, :], 0), axis=1)
    count = lax.dynamic_slice_in_dim(tile_count, own * TILES, TILES, 0)
    return sel.astype(jnp.int32), slot.astype(jnp.int32), count.astype(jnp.int32)


def body(
    video_query,
    video_key,
    video_value,
    video_grad,
    text_query,
    text_key,
    text_value,
    text_grad,
    tile_list,
    tile_count,
    text_mask,
):
    own = lax.axis_index("seq")
    x = lax.all_to_all(
        pack(video_key, video_value, video_query, video_grad), "head", 0, 0, tiled=True
    )
    sel, slot, count = tables(tile_list, tile_count, own)
    n = jnp.sum((text_mask > 0).astype(jnp.int32)).reshape(1)
    n_own = jnp.where(own == 0, n, 0)
    sel, slot, count, n, n_own = lax.optimization_barrier((sel, slot, count, n, n_own))
    text = (text_query, text_key, text_value)

    send0, send1 = send(sel, n_own, *text, x)
    got0 = lax.all_to_all(send0, "seq", 0, 0, tiled=True)
    send1, text_out = text_stats(own.reshape(1), got0, text_grad, send1)
    got = lax.all_to_all(send1, "seq", 0, 0, tiled=True)
    packed, back0, own0, both, text0 = video(
        True, slot, count, n, x, got0, text_key, text_value
    )
    back0 = lax.all_to_all(back0, "seq", 0, 0, tiled=True)
    tqg, tacc, dx = text_backward(n_own, got, *text, text_grad, x, own0)
    packed, both, own_grads = video(
        False,
        slot,
        count,
        n,
        x,
        got,
        text_key,
        text_value,
        tqg,
        tacc,
        text0,
        dx,
        packed,
        both,
    )
    back = lax.all_to_all(both, "seq", 0, 0, tiled=True)
    packed = combine(sel, back0, back, dx, own_grads, packed)

    gathered = text_sum(back, text_out)[None]
    for bit, mask in STEPS:
        theirs = swapped(gathered, mask)
        first = jnp.concatenate([gathered, theirs], axis=0)
        second = jnp.concatenate([theirs, gathered], axis=0)
        gathered = jnp.where((own & bit) == 0, first, second)
    text_rows = jnp.transpose(gathered, (1, 0, 2, 3)).reshape(4, TXT, W)

    attended_video, video_query_grad, video_key_grad, video_value_grad = unpack(
        lax.all_to_all(packed, "head", 0, 0, tiled=True)
    )
    return (
        attended_video,
        video_query_grad,
        video_key_grad,
        video_value_grad,
        text_rows[0],
        text_rows[1],
        text_rows[2],
        text_rows[3],
    )


def solution(mesh):
    tokens, heads = P(("seq", "head"), None), P(None, "head")
    return jax.shard_map(
        body,
        mesh=mesh,
        in_specs=(tokens,) * 4 + (heads,) * 4 + (P(),) * 3,
        out_specs=(tokens,) * 4 + (heads,) * 4,
        check_vma=False,
    )
```

```python
import functools

import jax
import jax.numpy as jnp
from jax import lax
from jax.experimental import pallas as pl
from jax.experimental.pallas import tpu as pltpu
from jax.sharding import PartitionSpec as P

HD = 128
TXT = 256
TILE = 128
KT = 8
MOST = 2
GROUPS = 16
HEADS = 8
TILES = 8
NH = 3
W = NH * HD
SLOTS = GROUPS * MOST
POOL = TILES + SLOTS
TROWS = TXT // GROUPS
TLOCAL = TILES * TILE
TCHUNKS = TLOCAL // 256 + 1
PAIR_ROWS = MOST * 2 * TILE
SEND_FIRST = PAIR_ROWS + 2 * TROWS
SEND_REST = PAIR_ROWS + TROWS
BACK_REST = PAIR_ROWS + 5 * TROWS
NF = 2
WF = NF * HD
WR = W - WF

NEGATIVE = -1e30
FACTOR = HD**-0.5
LOG2E = 1.4426950408889634
FACTOR2 = FACTOR * LOG2E
VMEM_LIMIT = 67043328

F32 = jnp.float32
BF16 = jnp.bfloat16
SMEM = pltpu.SMEM
ANY = pl.ANY


def dot_nt(a, b):
    return lax.dot_general(a, b, (((1,), (1,)), ((), ())), preferred_element_type=F32)


def dot_nn(a, b):
    return lax.dot_general(a, b, (((1,), (0,)), ((), ())), preferred_element_type=F32)


def dot_tn(a, b):
    return lax.dot_general(a, b, (((0,), (0,)), ((), ())), preferred_element_type=F32)


def params(**kw):
    return pltpu.CompilerParams(vmem_limit_bytes=VMEM_LIMIT, **kw)


def cost(flops, nbytes, exps=0):
    return pl.CostEstimate(
        flops=int(flops), bytes_accessed=int(nbytes), transcendentals=int(exps)
    )


def go(copies):
    for copy in copies:
        copy.start()
    return copies


def finish(copies):
    for copy in copies:
        copy.wait()


def columns(h):
    return pl.ds(h * W, W)


def pack_kernel(k_ref, v_ref, q_ref, g_ref, o_ref, rows, in_sems, out_sems):
    refs = (k_ref, v_ref, q_ref, g_ref)
    loads = go([pltpu.make_async_copy(refs[n], rows.at[n], in_sems.at[n]) for n in range(4)])
    stores = []
    for n in range(4):
        loads[n].wait()
        stores += go(
            [
                pltpu.make_async_copy(
                    rows.at[n, :, columns(h)], o_ref.at[h, n], out_sems.at[n, h]
                )
                for h in range(HEADS)
            ]
        )
    finish(stores)


def any_specs(n):
    return [pl.BlockSpec(memory_space=ANY)] * n


def pack(k, v, q, g):
    return pl.pallas_call(
        pack_kernel,
        in_specs=any_specs(4),
        out_specs=pl.BlockSpec(memory_space=ANY),
        out_shape=jax.ShapeDtypeStruct((HEADS, 4, TILE, W), BF16),
        scratch_shapes=[
            pltpu.VMEM((4, TILE, HEADS * W), BF16),
            pltpu.SemaphoreType.DMA((4,)),
            pltpu.SemaphoreType.DMA((4, HEADS)),
        ],
        compiler_params=params(),
        cost_estimate=cost(0, 8 * TILE * HEADS * W * 2),
        name="pack",
    )(k, v, q, g)


def unpack_kernel(x_ref, a_ref, b_ref, c_ref, d_ref, rows, in_sems, out_sems):
    refs = (a_ref, b_ref, c_ref, d_ref)
    loads = [
        go(
            [
                pltpu.make_async_copy(
                    x_ref.at[h, n], rows.at[n, :, columns(h)], in_sems.at[n, h]
                )
                for h in range(HEADS)
            ]
        )
        for n in range(4)
    ]
    stores = []
    for n in range(4):
        finish(loads[n])
        stores += go([pltpu.make_async_copy(rows.at[n], refs[n], out_sems.at[n])])
    finish(stores)


def unpack(x):
    return pl.pallas_call(
        unpack_kernel,
        in_specs=any_specs(1),
        out_specs=any_specs(4),
        out_shape=[jax.ShapeDtypeStruct((TILE, HEADS * W), BF16)] * 4,
        scratch_shapes=[
            pltpu.VMEM((4, TILE, HEADS * W), BF16),
            pltpu.SemaphoreType.DMA((4, HEADS)),
            pltpu.SemaphoreType.DMA((4,)),
        ],
        compiler_params=params(),
        cost_estimate=cost(0, 8 * TILE * HEADS * W * 2),
        name="unpack",
    )(x)


def picked(sel_ref, x_ref, o_ref, sems, lanes):
    return [
        pltpu.make_async_copy(
            x_ref.at[sel_ref[g * MOST + m], kv, :, lanes],
            o_ref.at[g, pl.ds((2 * m + kv) * TILE, TILE)],
            sems.at[g, 2 * m + kv],
        )
        for g in range(GROUPS)
        for m in range(MOST)
        for kv in range(2)
    ]


def text_chunk(x_ref, text_ref, which, c, lanes):
    if c < TCHUNKS - 1:
        return x_ref[2 * c : 2 * c + 2, which, :, lanes].reshape(256, HD)
    return text_ref[:, lanes]


def head_lanes(j):
    return pl.ds(pl.multiple_of(j * HD, HD), HD)


def whole(shape):
    return pl.BlockSpec(shape, lambda i: (0,) * len(shape))


TEXT = (TXT, W)
LOCAL_KV = (TILES, 2, TILE, W)


def thirds(x):
    first = x.astype(BF16).astype(F32)
    second = (x - first).astype(BF16).astype(F32)
    return first, second, x - first - second


def put(lane, block, at, column):
    return jnp.where(lane == at, column, block)


def take(lane, block, low, high, j):
    hit = (lane >= low) & (lane < high) & (lane % 8 == j)
    return jnp.sum(jnp.where(hit, block, 0.0), axis=1, keepdims=True)


def send_kernel(
    sel_ref,
    n_ref,
    tq_ref,
    tk_ref,
    tv_ref,
    x_ref,
    o_ref,
    rest_ref,
    s_ref,
    part_ref,
    sems,
    rest_sems,
    part_sem,
):
    def put_part(n, rows):
        at, lanes = n // 2 * TROWS, slice(n % 2 * HD, (n % 2 + 1) * HD)
        part_ref[:, at : at + TROWS, lanes] = rows.astype(BF16).reshape(GROUPS, TROWS, HD)

    tiles = go(picked(sel_ref, x_ref, o_ref, sems, pl.ds(0, WF)))
    tiles += go(picked(sel_ref, x_ref, rest_ref, rest_sems, pl.ds(WF, WR)))
    live = lax.broadcasted_iota(jnp.int32, (TXT, TXT), 1) < n_ref[0]
    lane = lax.broadcasted_iota(jnp.int32, (TXT, HD), 1)
    stats = jnp.zeros((TXT, HD), F32)
    for j in range(NH):
        lanes = slice(j * HD, (j + 1) * HD)
        query = tq_ref[:, lanes]
        top = None
        for c in range(TCHUNKS):
            s = dot_nt(query, text_chunk(x_ref, tk_ref, 0, c, lanes)) * FACTOR2
            if c == TCHUNKS - 1:
                s = jnp.where(live, s, NEGATIVE)
            s_ref[c] = s
            top = s if top is None else jnp.maximum(top, s)
        top = jnp.max(top, axis=1, keepdims=True).astype(BF16).astype(F32)
        total, out = None, None
        for c in range(TCHUNKS):
            p = jnp.exp2(s_ref[c] - top)
            part = dot_nn(p.astype(BF16), text_chunk(x_ref, tv_ref, 1, c, lanes))
            total = p if total is None else total + p
            out = part if out is None else out + part
        total = jnp.sum(total, axis=1, keepdims=True)
        put_part(j, out)
        stats = put(lane, stats, j, top)
        for n, third in enumerate(thirds(total)):
            stats = put(lane, stats, 8 * (n + 1) + j, third)
    put_part(NH, stats)
    parts = go(
        [pltpu.make_async_copy(part_ref, o_ref.at[:, pl.ds(PAIR_ROWS, 2 * TROWS)], part_sem)]
    )
    finish(tiles + parts)


def send(sel, n, tq, tk, tv, x):
    return pl.pallas_call(
        send_kernel,
        grid=(1,),
        in_specs=[pl.BlockSpec(memory_space=SMEM)] * 2 + [whole(TEXT)] * 3 + [whole(LOCAL_KV)],
        out_specs=any_specs(2),
        out_shape=[
            jax.ShapeDtypeStruct((GROUPS, SEND_FIRST, WF), BF16),
            jax.ShapeDtypeStruct((GROUPS, SEND_REST, WR), BF16),
        ],
        scratch_shapes=[
            pltpu.VMEM((TCHUNKS, TXT, 256), F32),
            pltpu.VMEM((GROUPS, 2 * TROWS, WF), BF16),
            pltpu.SemaphoreType.DMA((GROUPS, 2 * MOST)),
            pltpu.SemaphoreType.DMA((GROUPS, 2 * MOST)),
            pltpu.SemaphoreType.DMA,
        ],
        compiler_params=params(),
        cost_estimate=cost(4 * NH * TXT * TCHUNKS * 256 * HD, 5 << 20, NH * TXT * 1280),
        name="send",
    )(sel, n, tq, tk, tv, x)


def text_stats_kernel(own_ref, got_ref, tg_ref, in_ref, o_ref, out_ref, parts, tg, stats_ref, sems):
    mine = pl.ds(pl.multiple_of(own_ref[0] * TROWS, TROWS), TROWS)
    load = go(
        [
            pltpu.make_async_copy(
                got_ref.at[:, pl.ds(PAIR_ROWS, 2 * TROWS)], parts, sems.at[0]
            ),
            pltpu.make_async_copy(tg_ref.at[mine], tg, sems.at[1]),
        ]
    )
    lane_all = lax.broadcasted_iota(jnp.int32, (TXT, HD), 1)
    lane = lax.broadcasted_iota(jnp.int32, (TROWS, HD), 1)
    finish(load)
    received = parts[:, TROWS:, HD:].astype(F32).reshape(TXT, HD)
    stats = jnp.zeros((TROWS, HD), F32)
    for j in range(NH):
        lanes = slice(j * HD, (j + 1) * HD)
        tops = take(lane_all, received, 0, 8, j).reshape(GROUPS, TROWS, 1)
        totals = take(lane_all, received, 8, 32, j).reshape(GROUPS, TROWS, 1)
        top = jnp.max(tops, axis=0)
        scale = jnp.exp2(tops - top[None])
        total = jnp.sum(scale * totals, axis=0)
        part = parts[:, j // 2 * TROWS : (j // 2 + 1) * TROWS, j % 2 * HD : (j % 2 + 1) * HD]
        out = jnp.sum(scale * part.astype(F32), axis=0) / total
        out_ref[:, lanes] = out.astype(BF16)
        offset = jnp.sum(tg[:, lanes].astype(F32) * out, axis=1, keepdims=True)
        for n, third in enumerate(thirds(top + jnp.log2(total)) + thirds(offset)):
            stats = put(lane, stats, 8 * n + j, third)
    stats_ref[...] = jnp.broadcast_to(stats.astype(BF16)[None], (GROUPS, TROWS, HD))
    finish(
        go([pltpu.make_async_copy(stats_ref, o_ref.at[:, pl.ds(PAIR_ROWS, TROWS)], sems.at[2])])
    )


def text_stats(own, got, tg, send):
    return pl.pallas_call(
        text_stats_kernel,
        grid=(1,),
        in_specs=[pl.BlockSpec(memory_space=SMEM)] + any_specs(3),
        out_specs=[pl.BlockSpec(memory_space=ANY), whole((TROWS, W))],
        out_shape=[
            jax.ShapeDtypeStruct(send.shape, BF16),
            jax.ShapeDtypeStruct((TROWS, W), BF16),
        ],
        scratch_shapes=[
            pltpu.VMEM((GROUPS, 2 * TROWS, WF), BF16),
            pltpu.VMEM((TROWS, W), BF16),
            pltpu.VMEM((GROUPS, TROWS, WR), BF16),
            pltpu.SemaphoreType.DMA((3,)),
        ],
        input_output_aliases={3: 0},
        compiler_params=params(),
        cost_estimate=cost(TXT * W * 8, 1 << 19),
        name="text_stats",
    )(own, got, tg, send)


def text_backward_kernel(
    n_ref, got_ref, tq_ref, tk_ref, tv_ref, tg_ref, x_ref, own_ref, tqg_ref, acc_ref, dx_ref, rows, sem
):
    load = go(
        [
            pltpu.make_async_copy(
                got_ref.at[:, pl.ds(PAIR_ROWS, TROWS), pl.ds(0, HD)], rows, sem
            )
        ]
    )
    live = lax.broadcasted_iota(jnp.int32, (TXT, TXT), 1) < n_ref[0]
    lane = lax.broadcasted_iota(jnp.int32, (TXT, HD), 1)
    finish(load)

    def head(j, carry):
        lanes = head_lanes(j)
        stats = rows[...].astype(F32).reshape(TXT, HD)
        log_total = take(lane, stats, 0, 24, j)
        offset = take(lane, stats, 24, 48, j)
        query, grad = tq_ref[:, lanes], tg_ref[:, lanes]
        query_grad = None
        for c in range(TCHUNKS):
            key = text_chunk(x_ref, tk_ref, 0, c, lanes)
            value = text_chunk(x_ref, tv_ref, 1, c, lanes)
            s = dot_nt(query, key) * FACTOR2
            if c == TCHUNKS - 1:
                s = jnp.where(live, s, NEGATIVE)
            p = jnp.exp2(s - log_total)
            ds = (p * (dot_nt(grad, value) - offset)).astype(BF16)
            p = p.astype(BF16)
            part = dot_nn(ds, key)
            query_grad = part if query_grad is None else query_grad + part
            key_grad = dot_tn(ds, query)
            value_grad = dot_tn(p, grad)
            if c < TCHUNKS - 1:
                dx_ref[2 * c : 2 * c + 2, 0, :, lanes] = key_grad.reshape(2, TILE, HD)
                dx_ref[2 * c : 2 * c + 2, 1, :, lanes] = value_grad.reshape(2, TILE, HD)
            else:
                acc_ref[0, :, lanes] = key_grad
                acc_ref[1, :, lanes] = value_grad
        tqg_ref[:, lanes] = query_grad * FACTOR
        return carry

    lax.fori_loop(0, NH, head, 0)
    for t in range(TILES):
        dx_ref[t, :, :, :WF] += own_ref[t]


def text_backward(n, got, tq, tk, tv, tg, x, own):
    return pl.pallas_call(
        text_backward_kernel,
        grid=(1,),
        in_specs=[pl.BlockSpec(memory_space=SMEM)]
        + any_specs(1)
        + [whole(TEXT)] * 4
        + [whole(LOCAL_KV), whole((TILES, 2, TILE, WF))],
        out_specs=[whole(TEXT), whole((2, TXT, W)), whole(LOCAL_KV)],
        out_shape=[
            jax.ShapeDtypeStruct(TEXT, F32),
            jax.ShapeDtypeStruct((2, TXT, W), F32),
            jax.ShapeDtypeStruct(LOCAL_KV, F32),
        ],
        scratch_shapes=[
            pltpu.VMEM((GROUPS, TROWS, HD), BF16),
            pltpu.SemaphoreType.DMA,
        ],
        compiler_params=params(),
        cost_estimate=cost(10 * NH * TXT * TCHUNKS * 256 * HD, 8 << 20, NH * TXT * 1280),
        name="text_backward",
    )(n, got, tq, tk, tv, tg, x, own)


CHUNKS = KT // 2 + 1


def video_kernel(
    first, slot_ref, count_ref, n_ref, x_ref, got_ref, tk_ref, tv_ref, *refs
):
    if first:
        packed_ref, back_ref, own_ref, both_ref, text_ref = refs[:5]
        refs = refs[5:]
    else:
        tqg_ref, tacc_ref, text0_ref, dx_ref = refs[:4]
        packed_ref, both_ref, own_ref = refs[6:9]
        refs = refs[9:]
    keys, values, s_ref, p_ref, dk_acc, dv_acc, tk_acc, tv_acc, pool, qg, out_ref, stage = refs[:12]
    text_stage, kv_sems, got_sems, qg_sem, back_sems, own_sems, dx_sems, out_sems = refs[12:]
    base, heads = (0, NF) if first else (NF, NH - NF)
    mine = slice(base * HD, (base + heads) * HD)
    lanes = pl.ds(base * HD, heads * HD)

    def pool_rows(slot, kv):
        return pl.ds(pl.multiple_of((2 * slot + kv) * TILE, TILE), TILE)

    loads = [
        pltpu.make_async_copy(
            x_ref.at[t, kv, :, lanes], pool.at[pool_rows(t, kv)], kv_sems.at[t, kv]
        )
        for t in range(TILES)
        for kv in range(2)
    ]
    loads.append(pltpu.make_async_copy(x_ref.at[:, pl.ds(2, 2), :, lanes], qg, qg_sem))
    loads += [
        pltpu.make_async_copy(
            got_ref.at[g, pl.ds(0, PAIR_ROWS)],
            pool.at[pl.ds(2 * TILES * TILE + g * PAIR_ROWS, PAIR_ROWS)],
            got_sems.at[g],
        )
        for g in range(GROUPS)
    ]
    if not first:
        loads += [
            pltpu.make_async_copy(
                dx_ref.at[:, n, :, lanes], acc.at[pl.ds(0, TILES)], dx_sems.at[n]
            )
            for n, acc in enumerate((dk_acc, dv_acc))
        ]
    go(loads)
    keys[0] = tk_ref[:, mine]
    values[0] = tv_ref[:, mine]

    def clear(slot, carry):
        dk_acc[slot] = jnp.zeros((TILE, heads * HD), F32)
        dv_acc[slot] = jnp.zeros((TILE, heads * HD), F32)
        return carry

    lax.fori_loop(0 if first else TILES, POOL, clear, 0)
    if first:
        tk_acc[...] = jnp.zeros((TXT, heads * HD), F32)
        tv_acc[...] = jnp.zeros((TXT, heads * HD), F32)
    else:
        tk_acc[...] = tacc_ref[0, :, mine]
        tv_acc[...] = tacc_ref[1, :, mine]
    text_live = lax.broadcasted_iota(jnp.int32, (TXT, TILE), 0) < n_ref[0]
    finish(loads)
    cuts = [slice(h * HD, (h + 1) * HD) for h in range(heads)]

    def tile(i, carry):
        count = count_ref[i]

        def run(pairs):
            slots = [slot_ref[i * KT + e] for e in range(2 * pairs)]
            for e in range(2 * pairs):
                half = pl.ds((e % 2) * TILE, TILE)
                keys[1 + e // 2, half] = pool[pool_rows(slots[e], 0)]
                values[1 + e // 2, half] = pool[pool_rows(slots[e], 1)]
            query = [qg[i, 0, :, cut] for cut in cuts]
            grad = [qg[i, 1, :, cut] for cut in cuts]
            tops, scales, offsets = [], [], []
            for h, cut in enumerate(cuts):
                top = None
                for c in range(pairs + 1):
                    s = dot_nt(keys[c, :, cut], query[h]) * FACTOR2
                    if c == 0:
                        s = jnp.where(text_live, s, NEGATIVE)
                    elif c == pairs:
                        dead = jnp.where(2 * pairs <= count, s[TILE:], NEGATIVE)
                        s = jnp.concatenate([s[:TILE], dead], axis=0)
                    s_ref[h, c] = s
                    part = jnp.max(s.reshape(32, 8, TILE), axis=0)
                    top = part if top is None else jnp.maximum(top, part)
                tops.append(jnp.max(top, axis=0, keepdims=True))
            for h, cut in enumerate(cuts):
                total = None
                for c in range(pairs + 1):
                    p = jnp.exp2(s_ref[h, c] - tops[h])
                    s_ref[h, c] = p
                    part = jnp.sum(p.reshape(32, 8, TILE), axis=0)
                    total = part if total is None else total + part
                scales.append(1.0 / jnp.sum(total, axis=0, keepdims=True))
            for h, cut in enumerate(cuts):
                out = None
                for c in range(pairs + 1):
                    p = s_ref[h, c] * scales[h]
                    s_ref[h, c] = p
                    p = p.astype(BF16)
                    p_ref[h, c] = p
                    part = dot_tn(p, values[c, :, cut])
                    out = part if out is None else out + part
                out_ref[i, 0, :, cut] = out.astype(BF16)
                offsets.append(
                    jnp.sum((grad[h].astype(F32) * out).T, axis=0, keepdims=True)
                )
            for h, cut in enumerate(cuts):
                query_grad = None
                for c in range(pairs + 1):
                    dp = dot_nt(values[c, :, cut], grad[h])
                    ds = (s_ref[h, c] * (dp - offsets[h])).astype(BF16)
                    part = dot_tn(ds, keys[c, :, cut])
                    query_grad = part if query_grad is None else query_grad + part
                    key_grad = dot_nn(ds, query[h])
                    value_grad = dot_nn(p_ref[h, c], grad[h])
                    if c == 0:
                        tk_acc[:, cut] += key_grad
                        tv_acc[:, cut] += value_grad
                    else:
                        for e in (0, 1):
                            slot = slots[2 * (c - 1) + e]
                            rows = slice(e * TILE, (e + 1) * TILE)
                            dk_acc[slot, :, cut] += key_grad[rows]
                            dv_acc[slot, :, cut] += value_grad[rows]
                out_ref[i, 1, :, cut] = (query_grad * FACTOR).astype(BF16)

        for pairs in range(1, KT // 2 + 1):

            @pl.when((count + 1) // 2 == pairs)
            def _():
                run(pairs)

        return carry

    lax.fori_loop(0, TILES, tile, 0)

    stores = go(
        [
            pltpu.make_async_copy(acc.at[pl.ds(0, TILES)], own_ref.at[:, n], own_sems.at[n])
            for n, acc in enumerate((dk_acc, dv_acc))
        ]
        + [
            pltpu.make_async_copy(
                out_ref, packed_ref.at[:, pl.ds(0, 2), :, lanes], out_sems.at[0]
            )
        ]
    )
    if first:
        text_ref[0] = tk_acc[...]
        text_ref[1] = tv_acc[...]
    else:

        def store(n, values):
            at, cut = n // 2 * TROWS, slice(n % 2 * HD, (n % 2 + 1) * HD)
            values = values.reshape(GROUPS, TROWS, HD).astype(BF16)
            text_stage[:, at : at + TROWS, cut] = values

        for h in range(NH):
            cut = slice(h * HD, (h + 1) * HD)
            if h < NF:
                key_grad = tacc_ref[0, :, cut] + text0_ref[0, :, cut]
                value_grad = tacc_ref[1, :, cut] + text0_ref[1, :, cut]
            else:
                key_grad, value_grad = tk_acc[...], tv_acc[...]
            store(h, tqg_ref[:, cut])
            store(NH + h, key_grad * FACTOR)
            store(2 * NH + h, value_grad)
        store(3 * NH, jnp.zeros((TXT, HD), F32))
        stores += go(
            [
                pltpu.make_async_copy(
                    text_stage, both_ref.at[:, pl.ds(PAIR_ROWS, 5 * TROWS)], out_sems.at[1]
                )
            ]
        )
    pair_rows = pl.ds(0, PAIR_ROWS)
    for g in range(GROUPS):
        for m in range(MOST):
            slot = TILES + g * MOST + m
            stage[g, 2 * m * TILE : (2 * m + 1) * TILE] = (dk_acc[slot] * FACTOR).astype(BF16)
            stage[g, (2 * m + 1) * TILE : (2 * m + 2) * TILE] = dv_acc[slot].astype(BF16)
        if first:
            targets = (back_ref.at[g], both_ref.at[g, pair_rows, pl.ds(0, HD)])
        else:
            targets = (both_ref.at[g, pair_rows, pl.ds(HD, HD)],)
        stores += go(
            [
                pltpu.make_async_copy(
                    stage.at[g, :, pl.ds(n * HD, HD)], target, back_sems.at[g, n]
                )
                for n, target in enumerate(targets)
            ]
        )
    finish(stores)


def video(first, slot, count, n, x, got, tk, tv, *text):
    heads = NF if first else NH - NF
    width = heads * HD
    pair = (TILES, 2, TILE, width)
    in_specs = [pl.BlockSpec(memory_space=SMEM)] * 3 + any_specs(2) + [whole(TEXT)] * 2
    packed = jax.ShapeDtypeStruct((TILES, 4, TILE, W), BF16)
    both = jax.ShapeDtypeStruct((GROUPS, BACK_REST, 2 * HD), BF16)
    own = jax.ShapeDtypeStruct(pair, F32)
    if first:
        out_specs = any_specs(4) + [whole((2, TXT, WF))]
        back = jax.ShapeDtypeStruct((GROUPS, PAIR_ROWS, HD), BF16)
        out_shape = [packed, back, own, both, jax.ShapeDtypeStruct((2, TXT, WF), F32)]
        aliases = {}
    else:
        in_specs += [whole(TEXT), whole((2, TXT, W)), whole((2, TXT, WF))] + any_specs(3)
        out_specs = any_specs(3)
        out_shape = [packed, both, own]
        aliases = {11: 0, 12: 1}
    return pl.pallas_call(
        functools.partial(video_kernel, first),
        grid=(1,),
        in_specs=in_specs,
        out_specs=out_specs,
        out_shape=out_shape,
        scratch_shapes=[
            pltpu.VMEM((CHUNKS, 256, width), BF16),
            pltpu.VMEM((CHUNKS, 256, width), BF16),
            pltpu.VMEM((heads, CHUNKS, 256, TILE), F32),
            pltpu.VMEM((heads, CHUNKS, 256, TILE), BF16),
            pltpu.VMEM((POOL, TILE, width), F32),
            pltpu.VMEM((POOL, TILE, width), F32),
            pltpu.VMEM((TXT, width), F32),
            pltpu.VMEM((TXT, width), F32),
            pltpu.VMEM((POOL * 2 * TILE, width), BF16),
            pltpu.VMEM(pair, BF16),
            pltpu.VMEM(pair, BF16),
            pltpu.VMEM((GROUPS, PAIR_ROWS, width), BF16),
            pltpu.VMEM((GROUPS, 5 * TROWS, 2 * HD), BF16),
            pltpu.SemaphoreType.DMA((TILES, 2)),
            pltpu.SemaphoreType.DMA((GROUPS,)),
            pltpu.SemaphoreType.DMA,
            pltpu.SemaphoreType.DMA((GROUPS, 2)),
            pltpu.SemaphoreType.DMA((2,)),
            pltpu.SemaphoreType.DMA((2,)),
            pltpu.SemaphoreType.DMA((2,)),
        ],
        input_output_aliases=aliases,
        compiler_params=params(),
        cost_estimate=cost(
            12 * heads * TLOCAL * 1280 * HD, heads * (8 << 20), heads * TLOCAL * 1280
        ),
        name="video_first" if first else "video_rest",
    )(slot, count, n, x, got, tk, tv, *text)


def combine_kernel(
    sel_ref, first_ref, both_ref, dx_ref, own_ref, in_ref, packed_ref, acc, back, out, own_sems, sems, out_sem
):
    loads = go(
        [
            pltpu.make_async_copy(
                dx_ref.at[:, :, :, pl.ds(0, WF)], acc.at[:, :, :, pl.ds(0, WF)], own_sems.at[0]
            ),
            pltpu.make_async_copy(own_ref, acc.at[:, :, :, pl.ds(WF, WR)], own_sems.at[1]),
        ]
    )

    def parts(g):
        rows = pl.ds(0, PAIR_ROWS)
        return [
            pltpu.make_async_copy(first_ref.at[g], back.at[g, :, pl.ds(0, HD)], sems.at[g, 0]),
            pltpu.make_async_copy(
                both_ref.at[g, rows], back.at[g, :, pl.ds(HD, 2 * HD)], sems.at[g, 1]
            ),
        ]

    for g in range(GROUPS):
        go(parts(g))
    finish(loads)
    for t in range(TILES):
        acc[t, 0] = acc[t, 0] * FACTOR

    def add(g, carry):
        finish(parts(g))
        for m in range(MOST):
            at = sel_ref[g * MOST + m]
            part = back[g, 2 * m * TILE : 2 * (m + 1) * TILE].astype(F32)
            acc[at] += part.reshape(2, TILE, W)
        return carry

    lax.fori_loop(0, GROUPS, add, 0)
    for t in range(TILES):
        out[t] = acc[t].astype(BF16)
    finish(go([pltpu.make_async_copy(out, packed_ref.at[:, pl.ds(2, 2)], out_sem)]))


def combine(sel, first, both, dx, own, packed):
    return pl.pallas_call(
        combine_kernel,
        grid=(1,),
        in_specs=[pl.BlockSpec(memory_space=SMEM)] + any_specs(5),
        out_specs=pl.BlockSpec(memory_space=ANY),
        out_shape=jax.ShapeDtypeStruct((TILES, 4, TILE, W), BF16),
        scratch_shapes=[
            pltpu.VMEM(LOCAL_KV, F32),
            pltpu.VMEM((GROUPS, PAIR_ROWS, W), BF16),
            pltpu.VMEM(LOCAL_KV, BF16),
            pltpu.SemaphoreType.DMA((2,)),
            pltpu.SemaphoreType.DMA((GROUPS, 2)),
            pltpu.SemaphoreType.DMA,
        ],
        input_output_aliases={5: 0},
        compiler_params=params(),
        cost_estimate=cost(TLOCAL * W * 64, 14 << 20),
        name="combine",
    )(sel, first, both, dx, own, packed)


def text_sum_kernel(back_ref, out_ref, o_ref, rows, sem):
    load = [pltpu.make_async_copy(back_ref.at[:, pl.ds(PAIR_ROWS, 5 * TROWS)], rows, sem)]
    finish(go(load))
    total = jnp.sum(rows[...].astype(F32), axis=0).astype(BF16)
    o_ref[0] = out_ref[...]
    for n in range(3 * NH):
        h = n % NH
        at, cut = n // 2 * TROWS, slice(n % 2 * HD, (n % 2 + 1) * HD)
        o_ref[n // NH + 1, :, h * HD : (h + 1) * HD] = total[at : at + TROWS, cut]


def text_sum(back, out):
    return pl.pallas_call(
        text_sum_kernel,
        grid=(1,),
        in_specs=any_specs(1) + [whole((TROWS, W))],
        out_specs=whole((4, TROWS, W)),
        out_shape=jax.ShapeDtypeStruct((4, TROWS, W), BF16),
        scratch_shapes=[
            pltpu.VMEM((GROUPS, 5 * TROWS, 2 * HD), BF16),
            pltpu.SemaphoreType.DMA,
        ],
        compiler_params=params(),
        cost_estimate=cost(GROUPS * 9 * TROWS * WR, 1 << 20),
        name="text_sum",
    )(back, out)


def swapped(x, mask):
    return lax.ppermute(x, "seq", [(i, i ^ mask) for i in range(GROUPS)])


def tables(tile_list, tile_count, own):
    live = jnp.arange(KT)[None, :] < tile_count[:, None]
    listed = jnp.where(live, tile_list, -1)

    def ranked(wanted):
        before = jnp.arange(TILES)[:, None] < jnp.arange(TILES)[None, :]
        return jnp.sum(jnp.where(before[None], wanted[:, :, None], 0), axis=1)

    mine = own * TILES + jnp.arange(TILES)
    asked = jnp.any(
        listed.reshape(GROUPS, TILES * KT, 1) == mine[None, None, :], axis=1
    ).astype(jnp.int32)
    rank = ranked(asked)
    chosen = (asked[:, None, :] > 0) & (rank[:, None, :] == jnp.arange(MOST)[None, :, None])
    sel = jnp.sum(jnp.where(chosen, jnp.arange(TILES)[None, None, :], 0), axis=2).reshape(SLOTS)

    my_list = lax.dynamic_slice_in_dim(listed, own * TILES, TILES, 0).reshape(TILES * KT)
    hits = my_list[:, None] == jnp.arange(GROUPS * TILES)[None, :]
    needed = jnp.any(hits, axis=0).astype(jnp.int32).reshape(GROUPS, TILES)
    where_to = TILES + jnp.arange(GROUPS)[:, None] * MOST + jnp.minimum(ranked(needed), MOST - 1)
    local = jnp.arange(GROUPS)[:, None] == own
    where_to = jnp.where(local, jnp.arange(TILES)[None, :], where_to).reshape(GROUPS * TILES)
    slot = jnp.sum(jnp.where(hits, where_to[None, :], 0), axis=1)
    count = lax.dynamic_slice_in_dim(tile_count, own * TILES, TILES, 0)
    return sel.astype(jnp.int32), slot.astype(jnp.int32), count.astype(jnp.int32)


def body(
    video_query,
    video_key,
    video_value,
    video_grad,
    text_query,
    text_key,
    text_value,
    text_grad,
    tile_list,
    tile_count,
    text_mask,
):
    own = lax.axis_index("seq")
    x = lax.all_to_all(
        pack(video_key, video_value, video_query, video_grad), "head", 0, 0, tiled=True
    )
    sel, slot, count = tables(tile_list, tile_count, own)
    n = jnp.sum((text_mask > 0).astype(jnp.int32)).reshape(1)
    n_own = jnp.where(own == 0, n, 0)
    sel, slot, count, n, n_own = lax.optimization_barrier((sel, slot, count, n, n_own))
    text = (text_query, text_key, text_value)

    send0, send1 = send(sel, n_own, *text, x)
    got0 = lax.all_to_all(send0, "seq", 0, 0, tiled=True)
    send1, text_out = text_stats(own.reshape(1), got0, text_grad, send1)
    got = lax.all_to_all(send1, "seq", 0, 0, tiled=True)
    packed, back0, own0, both, text0 = video(
        True, slot, count, n, x, got0, text_key, text_value
    )
    back0 = lax.all_to_all(back0, "seq", 0, 0, tiled=True)
    tqg, tacc, dx = text_backward(n_own, got, *text, text_grad, x, own0)
    packed, both, own_grads = video(
        False,
        slot,
        count,
        n,
        x,
        got,
        text_key,
        text_value,
        tqg,
        tacc,
        text0,
        dx,
        packed,
        both,
    )
    both, back0 = lax.optimization_barrier((both, back0))
    back = lax.all_to_all(both, "seq", 0, 0, tiled=True)

    def exchanged(gathered, bit, theirs):
        first = jnp.concatenate([gathered, theirs], axis=0)
        second = jnp.concatenate([theirs, gathered], axis=0)
        return jnp.where((own & bit) == 0, first, second)

    rows = text_sum(back, text_out)[None]
    theirs = swapped(rows, 8)
    packed = combine(sel, back0, back, dx, own_grads, packed)
    packed, theirs = lax.optimization_barrier((packed, theirs))
    gathered = exchanged(rows, 8, theirs)
    for bit, mask in ((1, 1), (2, 2), (4, 6)):
        gathered = exchanged(gathered, bit, swapped(gathered, mask))
    gathered = gathered.reshape(2, 2, 2, 2, 4, TROWS, W)
    text_rows = jnp.transpose(gathered, (4, 3, 0, 1, 2, 5, 6)).reshape(4, TXT, W)

    attended_video, video_query_grad, video_key_grad, video_value_grad = unpack(
        lax.all_to_all(packed, "head", 0, 0, tiled=True)
    )
    return (
        attended_video,
        video_query_grad,
        video_key_grad,
        video_value_grad,
        text_rows[0],
        text_rows[1],
        text_rows[2],
        text_rows[3],
    )


def solution(mesh):
    tokens, heads = P(("seq", "head"), None), P(None, "head")
    return jax.shard_map(
        body,
        mesh=mesh,
        in_specs=(tokens,) * 4 + (heads,) * 4 + (P(),) * 3,
        out_specs=(tokens,) * 4 + (heads,) * 4,
        check_vma=False,
    )
```
